32 devices in a mesh: tm: 4 (over y, x), space: 8 (over z, core).
Axes of the slice: x: 2, y: 2, z: 4, core: 2. Of those that a mesh axis runs over, the one named last changes fastest.
Arguments:
- source: float32 [8, 2048, 128], P('tm', 'space'), may hold values from -6 to 6
- elem_scale: float32 [2048], P('space'), may hold values from 1 to 2
- diag_block: float32 [128, 128], replicated, as said below
- block_inverse: float32 [128, 128], replicated, as said below
- face_flux: float32 [4, 128, 128], replicated, may hold values from -0.072 to 0.072
- time_trace: float32 [128, 128], replicated, as said below
- neighbours: int32 [2048, 4], P('space'), may hold values from 0 to 287, as said below
- send_rows: int32 [8, 32], P('space'), may hold values from 0 to 255, as said below
Outputs:
- smoothed: float32 [8, 2048, 128], P('tm', 'space')
The draws below stay inside these ranges and needn't reach their ends.
Inputs may be any that keep to these rules, and one draw needn't show every extreme that they name: `neighbours`: indexes the extended list of the element's own partition, of 288 positions; each of the 32 received positions is named by exactly one face of the partition's elements, and only the partition's sent elements name received positions. `send_rows`: each row holds 32 distinct local positions of its partition's elements. `diag_block`: the identity plus a skew-symmetric matrix plus a positive semidefinite matrix. `block_inverse`: the inverse of diag_block. `time_trace`: its largest singular value is at most 0.9.
All inputs are finite; a program needn't handle non-finite values.
Results may differ from the reference program's by a relative error of at most 0.0001.
Values sent between devices are 32-bit elements; how exact they have to be, the bound alone decides.
No kernel may reach another device: no remote copies, remote signals or barrier semaphores. Data moves between devices by JAX's collectives and lax.ppermute only.
A program may use at most 64 MiB of HBM per device.

```python
import math
import jax
import jax.numpy as jnp
from jax import lax

U = 128
E_DEV = 256
HB = 16
NT = 8
NE = 2048


def skew_part(key, number):
    first = jax.random.normal(jax.random.fold_in(key, number), (U, U), jnp.float32) * (0.3 / math.sqrt(U))
    return (first - first.T) / math.sqrt(2.0)


def block_pair(key):
    skew = skew_part(key, 11)
    second = jax.random.normal(jax.random.fold_in(key, 12), (U, U), jnp.float32)
    diffusion = jnp.dot(second, second.T) * (0.1 / U)
    block = jnp.eye(U, dtype=jnp.float32) + skew + diffusion
    return (block, jnp.linalg.inv(block))


def draw_diag_block(key, part):
    return block_pair(key)[0]


def draw_block_inverse(key, part):
    return block_pair(key)[1]


def draw_time_trace(key, part):
    skew = skew_part(key, 21)
    return 0.9 * jnp.linalg.inv(jnp.eye(U, dtype=jnp.float32) + skew)


def shuffle_one(subkey):
    return jax.random.permutation(subkey, E_DEV).astype(jnp.int32)


def place_value(order, value, slot):
    held = order[slot]
    order = jnp.where(order == value, held, order)
    return order.at[slot].set(value)


def fix_order(order):
    order = place_value(order, E_DEV - 1, 0)
    return place_value(order, 0, HB)


def rank_of(order):
    return jnp.zeros((E_DEV,), jnp.int32).at[order].set(jnp.arange(E_DEV, dtype=jnp.int32))


def boundary_layout(key):
    partitions = NE // E_DEV
    key_list = jax.random.split(jax.random.fold_in(key, 31), partitions)
    orders = jax.vmap(shuffle_one)(key_list)
    chosen = jax.random.randint(jax.random.fold_in(key, 32), (), 0, partitions)
    fixed = jax.vmap(fix_order)(orders)
    pick = jnp.arange(partitions, dtype=jnp.int32)[:, None] == chosen
    orders = jnp.where(pick, fixed, orders).astype(jnp.int32)
    ranks = jax.vmap(rank_of)(orders)
    return (orders, ranks)


def draw_send_rows(key, part):
    orders, ranks = boundary_layout(key)
    return orders[:, :2 * HB].astype(jnp.int32)


def draw_neighbours(key, part):
    partitions = NE // E_DEV
    orders, ranks = boundary_layout(key)
    columns = []
    for face_index in range(4):
        key_list = jax.random.split(jax.random.fold_in(key, 40 + face_index), partitions)
        columns.append(jax.vmap(shuffle_one)(key_list))
    received = (E_DEV + ranks).astype(jnp.int32)
    columns[2] = jnp.where(ranks < HB, received, columns[2])
    columns[3] = jnp.where((ranks >= HB) & (ranks < 2 * HB), received, columns[3])
    stacked = jnp.stack(columns, axis=-1)
    return stacked.reshape(NE, 4).astype(jnp.int32)


def levels(stream_key, extent, cuts, least, top_value):
    gain = 1.0
    for dim, blocks in cuts:
        steps = jax.random.uniform(jax.random.fold_in(jax.random.fold_in(stream_key, 6), dim), (blocks,), jnp.float32, least / len(cuts), top_value / len(cuts))
        gain = gain * jnp.repeat(jnp.exp(steps), extent[dim] // blocks).reshape((-1,) + (1,) * (len(extent) - 1 - dim))
    return gain


def normal_values(key, dims, scale, most, pieces=(), held_as=jnp.bfloat16):
    array = jax.random.normal(key, dims, jnp.float32) * scale
    if len(pieces) > 0:
        array = levels(key, dims, pieces, -0.22, 0.18) * array
    return jnp.clip(array, min=-most, max=most).astype(held_as)


def setup_inputs(seed: int = 0) -> dict:
    arg_keys = jax.random.split(jax.random.key(seed), 9)
    source = normal_values(arg_keys[0], (NT, NE, U), 1.0, 6.0, ((0, 4), (1, 8)), jnp.float32)
    elem_scale = jnp.clip(jnp.exp(math.log(2.0) - 0.6931472 * jax.random.uniform(arg_keys[1], (NE,), jnp.float32) ** levels(arg_keys[1], (NE,), ((0, 8),), -0.2, 0.2)), 1.0, 2.0)
    diag_block = draw_diag_block(jax.random.fold_in(arg_keys[8], 71), 0)
    block_inverse = draw_block_inverse(jax.random.fold_in(arg_keys[8], 71), 0)
    face_flux = normal_values(arg_keys[4], (4, U, U), 0.012, 0.072, (), jnp.float32)
    time_trace = draw_time_trace(jax.random.fold_in(arg_keys[8], 71), 0)
    neighbours = draw_neighbours(jax.random.fold_in(arg_keys[8], 71), 0)
    send_rows = draw_send_rows(jax.random.fold_in(arg_keys[8], 71), 0)
    return {"source": source, "elem_scale": elem_scale, "diag_block": diag_block, "block_inverse": block_inverse, "face_flux": face_flux, "time_trace": time_trace, "neighbours": neighbours, "send_rows": send_rows}


DAMPING = 0.7

def product(left, right):
    return jnp.dot(left.astype(jnp.float32), right.astype(jnp.float32), precision=lax.Precision.HIGHEST, preferred_element_type=jnp.float32)

def reference(source, elem_scale, diag_block, block_inverse, face_flux, time_trace, neighbours, send_rows):
    partitions = NE // E_DEV
    halo_rows = HB
    face_ids = neighbours.reshape(partitions, E_DEV, 4)
    inv_scale = 1.0 / elem_scale

    def apply_slab(slab_pair):
        current, before = slab_pair
        blocks = current.reshape(partitions, E_DEV, U)
        outgoing = jnp.take_along_axis(blocks, send_rows[:, :, None], axis=1)
        from_left = jnp.roll(outgoing[:, halo_rows:], 1, axis=0)
        from_right = jnp.roll(outgoing[:, :halo_rows], -1, axis=0)
        extended = jnp.concatenate([blocks, from_left, from_right], axis=1)
        face_term = jnp.zeros((NE, U), jnp.float32)
        for face_index in range(4):
            picked = jnp.take_along_axis(extended, face_ids[:, :, face_index][:, :, None], axis=1)
            face_term = face_term + product(picked.reshape(NE, U), face_flux[face_index])
        diagonal_term = product(current, diag_block) * elem_scale[:, None]
        return diagonal_term - product(before, time_trace) - face_term

    def operate(field):
        earlier = jnp.concatenate([jnp.zeros_like(field[:1]), field[:-1]], axis=0)
        return lax.map(apply_slab, (field, earlier))

    def smooth(solution):
        residual = source - operate(solution)
        return solution + DAMPING * product(residual, block_inverse) * inv_scale[None, :, None]
    solution = DAMPING * product(source, block_inverse) * inv_scale[None, :, None]
    solution = smooth(solution)
    residual = source - operate(solution)
    coarse_rhs = residual.reshape(NT // 2, 2, NE, U)
    coarse_rhs = coarse_rhs[:, 0] + coarse_rhs[:, 1]
    coarse_scale = 1.0 / (2.0 * elem_scale - 1.0)

    def coarse_step(state, rhs_slab):
        state = coarse_scale[:, None] * product(rhs_slab + product(state, time_trace), block_inverse)
        return (state, state)
    zero_state = jnp.zeros((NE, U), jnp.float32)
    final_state, correction = lax.scan(coarse_step, zero_state, coarse_rhs)
    solution = solution + jnp.repeat(correction, 2, axis=0)
    solution = smooth(solution)
    solution = smooth(solution)
    return solution
```

```python
import jax
import jax.numpy as jnp
from jax import lax
from jax.experimental import pallas as pl
from jax.experimental.pallas import tpu as pltpu
from jax.sharding import PartitionSpec as P

DAMPING = 0.7
F32 = jnp.float32
BF16 = jnp.bfloat16
VMEM = pltpu.VMEM
SMEM = pltpu.SMEM

W_DIAG, W_FACE, W_SOURCE_TIME, W_TIME = 0, 1, 5, 6


def call(kernel, out_shapes, args, spaces=None, scratch=(), flops=4e8):
    spaces = spaces or [VMEM] * len(args)
    return pl.pallas_call(
        kernel,
        out_shape=[jax.ShapeDtypeStruct(s, d) for s, d in out_shapes],
        in_specs=[pl.BlockSpec(memory_space=s) for s in spaces],
        out_specs=[pl.BlockSpec(memory_space=VMEM)] * len(out_shapes),
        scratch_shapes=list(scratch),
        compiler_params=pltpu.CompilerParams(vmem_limit_bytes=24 << 20),
        cost_estimate=pl.CostEstimate(flops=int(flops), bytes_accessed=1 << 20, transcendentals=0),
    )(*args)


def split(x):
    head = x.astype(BF16)
    tail = (x - head.astype(F32)).astype(BF16)
    return jnp.concatenate([head, tail], axis=1)


def halves(x):
    width = x.shape[1] // 2
    return x[:, :width] + x[:, width:]


def dot(left, right):
    return jnp.dot(left, right, preferred_element_type=F32)


def dot32(left, right):
    return jnp.dot(left, right, precision=lax.Precision.HIGHEST, preferred_element_type=F32)


def product(parts, tile):
    return halves(dot(parts, tile))


def weight_tile(w):
    head = w.astype(BF16)
    tail = (w - head.astype(F32)).astype(BF16)
    top = jnp.concatenate([head, tail], axis=1)
    low = jnp.concatenate([head, jnp.zeros_like(head)], axis=1)
    return jnp.concatenate([top, low], axis=0)


def column(row, width):
    return jnp.transpose(jnp.broadcast_to(row, (width, row.shape[1])))


def own_faces(faces, pick_ref, weights_ref, parts):
    count = len(parts)
    width = parts[0].shape[1]
    rows = parts[0].shape[0]
    every = jnp.concatenate(parts, axis=1) if count > 1 else parts[0]
    sums = [None] * count
    for face in range(faces):
        picked = dot(pick_ref[face * rows : (face + 1) * rows, :], every).astype(BF16)
        for i in range(count):
            term = dot(picked[:, i * width : (i + 1) * width], weights_ref[W_FACE + face])
            sums[i] = term if sums[i] is None else sums[i] + term
    return [halves(s) for s in sums]


def arrived(from_e, from_o, count):
    even = lax.axis_index("space") % 2 == 0
    left = jnp.where(even, from_o[...], from_e[...])
    right = jnp.where(even, from_e[...], from_o[...])
    rows = left.shape[0] // count
    return [
        jnp.concatenate([left[i * rows : (i + 1) * rows], right[i * rows : (i + 1) * rows]], axis=0)
        for i in range(count)
    ]


def far_faces(faces, rows_in, weights_ref):
    count = len(rows_in)
    n = rows_in[0].shape[0]
    parts = split(jnp.concatenate(rows_in, axis=0) if count > 1 else rows_in[0])
    per_face = [product(parts, weights_ref[W_FACE + f]) for f in range(faces)]
    lanes = [
        split(jnp.concatenate([u[i * n : (i + 1) * n] for u in per_face], axis=0))
        for i in range(count)
    ]
    return jnp.concatenate(lanes, axis=1) if count > 1 else lanes[0]


def spread(select, table, count):
    total = dot(select, table)
    width = total.shape[1] // count
    return [halves(total[:, i * width : (i + 1) * width]) for i in range(count)]


def put_sent(e_ref, o_ref, slabs):
    rows = slabs[0].shape[0] // 2
    for i, s in enumerate(slabs):
        e_ref[i * rows : (i + 1) * rows, :] = s[:rows]
        o_ref[i * rows : (i + 1) * rows, :] = s[rows:]


def at_sent(sent_ref, values):
    every = jnp.concatenate([split(v) for v in values], axis=1)
    return spread(sent_ref[...], every, len(values))


def body(
    source, elem_scale, diag_block, block_inverse, face_flux, time_trace, neighbours, send_rows
):
    slabs, elements, width = source.shape
    faces = neighbours.shape[1]
    sent = send_rows.shape[1]
    halo = sent // 2
    groups = lax.axis_size("tm")
    ring = lax.axis_size("space")
    flat = source.reshape(slabs * elements, width)
    scale_row = elem_scale.reshape(1, elements)
    faces_row = neighbours.T
    stack = W_TIME + groups - 1
    full = ((elements, width), F32)
    two = ((slabs * elements, width), F32)
    edge = ((slabs * halo, width), F32)
    far = faces * sent

    swap_e = [(i, i ^ 1) for i in range(ring)]
    swap_o = [(i, (i + 1) % ring if i % 2 else (i - 1) % ring) for i in range(ring)]

    def exchange(to_e, to_o):
        return lax.ppermute(to_e, "space", swap_e), lax.ppermute(to_o, "space", swap_o)

    def later(x, by):
        return lax.ppermute(x, "tm", [(i, (i + by) % groups) for i in range(groups)])

    def sent_at(send_ref, i):
        first = jnp.where(lax.axis_index("space") % 2 == 0, halo, 0)
        return send_ref[0, lax.rem(first + i, sent)]

    def first_kernel(s_ref, scale_ref, inv_ref, send_ref, e_ref, o_ref, x_ref, g_ref):
        sigma = DAMPING / column(scale_ref[...], width)
        for t in range(slabs):
            x_ref[t * elements : (t + 1) * elements, :] = (
                s_ref[t * elements : (t + 1) * elements, :] * sigma
            )
        for i in range(sent):
            at = sent_at(send_ref, i)
            base = (i // halo) * slabs * halo + i % halo
            for t in range(slabs):
                g_ref[base + t * halo : base + t * halo + 1, :] = x_ref[
                    pl.ds(t * elements + at, 1), :
                ]
        out = dot32(g_ref[...], inv_ref[...])
        e_ref[...] = out[: slabs * halo]
        o_ref[...] = out[slabs * halo :]

    e0, o0 = call(
        first_kernel,
        [edge, edge],
        [flat, scale_row, block_inverse, send_rows],
        spaces=[VMEM, VMEM, VMEM, SMEM],
        scratch=[VMEM((slabs * elements, width), F32), VMEM((slabs * sent, width), F32)],
        flops=1e7,
    )
    before = later(source[-1], 1)
    re0, ro0 = exchange(e0, o0)

    def setup_kernel(
        s_ref, scale_ref, d_ref, inv_ref, f_ref, t_ref, nbr_ref, send_ref,
        v_ref, part_ref, psent_ref, sigs_ref, w_ref, pick_ref, q_ref, qs_ref, sent_ref,
        sig_ref, frac_ref, rows_ref,
    ):
        inv = inv_ref[...]
        trace = dot32(t_ref[...], inv)
        w_ref[W_DIAG] = weight_tile(dot32(d_ref[...], inv))
        for f in range(faces):
            w_ref[W_FACE + f] = weight_tile(dot32(f_ref[f], inv))
        w_ref[W_SOURCE_TIME] = weight_tile(dot32(inv, trace))
        power = trace
        for a in range(groups - 1):
            w_ref[W_TIME + a] = weight_tile(power)
            if a < groups - 2:
                power = dot32(power, trace)
        scale = column(scale_ref[...], width)
        sigma = DAMPING / scale
        sig_ref[...] = sigma
        frac_ref[...] = 1.0 / (2.0 * scale - 1.0)
        lane = lax.broadcasted_iota(jnp.int32, (elements, elements), 1)
        spot = lax.broadcasted_iota(jnp.int32, (elements, far), 1)
        wanted = jnp.zeros((elements, far), jnp.int32)
        for f in range(faces):
            wide = column(nbr_ref[f : f + 1, :], elements)
            pick_ref[f * elements : (f + 1) * elements, :] = jnp.where(
                wide == lane, 1.0, 0.0
            ).astype(BF16)
            wanted = jnp.where(spot // sent == f, column(nbr_ref[f : f + 1, :], far), wanted)
        q = jnp.where(wanted == elements + spot % sent, 1.0, 0.0).astype(BF16)
        q_ref[...] = q
        strip = lax.broadcasted_iota(jnp.int32, (1, elements), 1)
        for i in range(sent):
            rows_ref[i : i + 1, :] = jnp.where(strip == sent_at(send_ref, i), 1.0, 0.0)
        chosen = rows_ref[...].astype(BF16)
        sent_ref[...] = chosen
        qs_ref[...] = dot(chosen, q).astype(BF16)
        head = weight_tile(inv)
        v = [
            sigma * product(split(s_ref[t * elements : (t + 1) * elements, :]), head)
            for t in range(slabs)
        ]
        cut = [split(x) for x in v]
        near = own_faces(faces, pick_ref, w_ref, cut)
        parts = []
        for t in range(slabs):
            term = near[t]
            if t:
                term = term + product(cut[t - 1], w_ref[W_TIME])
            parts.append(
                2.0 * v[t] - DAMPING * product(cut[t], w_ref[W_DIAG]) + sigma * term
            )
            v_ref[t * elements : (t + 1) * elements, :] = v[t]
            part_ref[t * elements : (t + 1) * elements, :] = parts[t]
        got = at_sent(sent_ref, parts + [sigma])
        for t in range(slabs):
            psent_ref[t * sent : (t + 1) * sent, :] = got[t]
        sigs_ref[...] = got[slabs]

    (
        v0, part1, psent1, sig_sent, weights, pick, q_all, q_sent, choose, sigma_all, frac_all,
    ) = call(
        setup_kernel,
        [
            two, two, ((slabs * sent, width), F32), ((sent, width), F32),
            ((stack, 2 * width, 2 * width), BF16), ((faces * elements, elements), BF16),
            ((elements, far), BF16), ((sent, far), BF16), ((sent, elements), BF16), full, full,
        ],
        [
            flat, scale_row, diag_block, block_inverse, face_flux, time_trace, faces_row,
            send_rows,
        ],
        spaces=[VMEM] * 7 + [SMEM],
        scratch=[VMEM((sent, elements), F32)],
        flops=2e9,
    )

    def time_mask(x, by=1):
        return jnp.where(lax.axis_index("tm") >= by, x, jnp.zeros_like(x))

    def edge_one(
        re_ref, ro_ref, b_ref, psent_ref, sigs_ref, w_ref, qs_ref, sent_ref, e_ref, o_ref
    ):
        table = far_faces(faces, arrived(re_ref, ro_ref, slabs), w_ref)
        add = spread(qs_ref[...], table, slabs)
        picked = dot(sent_ref[...], split(b_ref[...])).astype(BF16)
        old = time_mask(product(picked, w_ref[W_SOURCE_TIME]))
        sig = sigs_ref[...]
        new = [psent_ref[t * sent : (t + 1) * sent, :] + sig * add[t] for t in range(slabs)]
        new[0] = new[0] + sig * sig * old
        put_sent(e_ref, o_ref, new)

    e1, o1 = call(
        edge_one,
        [edge, edge],
        [re0, ro0, before, psent1, sig_sent, weights, q_sent, choose],
        flops=1e7,
    )
    re1, ro1 = exchange(e1, o1)

    def middle(
        re_ref, ro_ref, b_ref, part_ref, v_ref, w_ref, pick_ref, q_ref, sig_ref, frac_ref,
        v1_ref, pa_ref, pb_ref, wp_ref, x_ref,
    ):
        sigma = sig_ref[...]
        frac = frac_ref[...]
        add = spread(q_ref[...], far_faces(faces, arrived(re_ref, ro_ref, slabs), w_ref), slabs)
        old = time_mask(product(split(b_ref[...]), w_ref[W_SOURCE_TIME]))
        va = part_ref[:elements, :] + sigma * add[0] + sigma * sigma * old
        vb = part_ref[elements:, :] + sigma * add[1]
        v0a, v0b = v_ref[:elements, :], v_ref[elements:, :]
        v1_ref[...] = vb
        ca, cb = split(va), split(vb)
        ga, gb = own_faces(faces, pick_ref, w_ref, [ca, cb])
        da, db = product(ca, w_ref[W_DIAG]), product(cb, w_ref[W_DIAG])
        ta, tb = product(ca, w_ref[W_TIME]), product(cb, w_ref[W_TIME])
        pa_ref[...] = va + v0a - DAMPING * da + sigma * ga
        pb_ref[...] = vb + v0b - DAMPING * db + sigma * (ta + gb)
        wp_ref[...] = (
            frac * (((v0a + v0b) - DAMPING * (da + db)) / sigma + ta + ga + gb) + vb
        )
        x_ref[...] = v0b + sigma * (ta - tb)

    v1b, pa0, pb0, wp, x_own = call(
        middle,
        [full] * 5,
        [re0, ro0, before, part1, v0, weights, pick, q_all, sigma_all, frac_all],
        flops=2e9,
    )

    def coarse_kernel(
        re_ref, ro_ref, wp_ref, pa_ref, pb_ref, w_ref, q_ref, sig_ref, frac_ref,
        w_out, pa_out, pb_out,
    ):
        add = spread(q_ref[...], far_faces(faces, arrived(re_ref, ro_ref, slabs), w_ref), slabs)
        w_out[...] = wp_ref[...] + frac_ref[...] * (add[0] + add[1])
        pa_out[...] = pa_ref[...] + sig_ref[...] * add[0]
        pb_out[...] = pb_ref[...] + sig_ref[...] * add[1]

    w_own, pa1, pb1 = call(
        coarse_kernel,
        [full] * 3,
        [re1, ro1, wp, pa0, pb0, weights, q_all, sigma_all, frac_all],
        flops=1e7,
    )
    earlier = [later(w_own, a) for a in range(1, groups)]
    x_before = later(x_own, 1)

    def recur(*refs):
        olds = refs[: groups - 1]
        w_own_ref, v1_ref, w_ref, sent_ref, frac_ref, c_ref, d_ref, e_ref, o_ref = refs[
            groups - 1 :
        ]
        frac = frac_ref[...]
        d = time_mask(olds[0][...])
        c = w_own_ref[...] - v1_ref[...]
        power = frac
        for a in range(1, groups):
            cut = split(time_mask(power * olds[a - 1][...], a))
            c = c + product(cut, w_ref[W_TIME + a - 1])
            if a < groups - 1:
                cut = split(time_mask(power * olds[a][...], a + 1))
                d = d + product(cut, w_ref[W_TIME + a - 1])
                power = power * frac
        c_ref[...] = c
        d_ref[...] = d
        put_sent(e_ref, o_ref, at_sent(sent_ref, [c, d]))

    c_all, d_all, e2, o2 = call(
        recur,
        [full, full, edge, edge],
        [*earlier, w_own, v1b, weights, choose, frac_all],
        flops=1e8,
    )
    re2, ro2 = exchange(e2, o2)

    def second(
        c_in, d_in, xb_ref, pa_ref, pb_ref, w_ref, pick_ref, sig_ref, sent_ref,
        a_ref, b_ref, z_ref, ps_ref,
    ):
        sigma = sig_ref[...]
        c, d = c_in[...], d_in[...]
        cc, cd = split(c), split(d)
        gc, gd = own_faces(faces, pick_ref, w_ref, [cc, cd])
        same = c - DAMPING * product(cc, w_ref[W_DIAG]) + sigma * gc
        td = product(cd, w_ref[W_TIME])
        a = pa_ref[...] + same + sigma * td
        b = pb_ref[...] + same + sigma * product(cc, w_ref[W_TIME])
        a_ref[...] = a
        b_ref[...] = b
        z_ref[...] = (
            time_mask(xb_ref[...]) + d - DAMPING * product(cd, w_ref[W_DIAG]) + sigma * (td + gd)
        )
        got = at_sent(sent_ref, [a, b])
        for t in range(slabs):
            ps_ref[t * sent : (t + 1) * sent, :] = got[t]

    a3, b3, z3, psent3 = call(
        second,
        [full, full, full, ((slabs * sent, width), F32)],
        [c_all, d_all, x_before, pa1, pb1, weights, pick, sigma_all, choose],
        flops=2e9,
    )

    def edge_two(re_ref, ro_ref, psent_ref, sigs_ref, w_ref, qs_ref, e_ref, o_ref):
        table = far_faces(faces, arrived(re_ref, ro_ref, 2)[:1], w_ref)
        add = sigs_ref[...] * spread(qs_ref[...], table, 1)[0]
        put_sent(
            e_ref, o_ref, [psent_ref[t * sent : (t + 1) * sent, :] + add for t in range(slabs)]
        )

    e3, o3 = call(
        edge_two,
        [edge, edge],
        [re2, ro2, psent3, sig_sent, weights, q_sent],
        flops=1e7,
    )
    re3, ro3 = exchange(e3, o3)

    def third(
        re_ref, ro_ref, a_in, b_in, z_in, v_ref, w_ref, pick_ref, q_ref, sig_ref, out_ref
    ):
        sigma = sig_ref[...]
        add = spread(q_ref[...], far_faces(faces, arrived(re_ref, ro_ref, 2), w_ref), 2)
        a = a_in[...] + sigma * add[0]
        b = b_in[...] + sigma * add[0]
        z = z_in[...] + sigma * add[1]
        ca, cb = split(a), split(b)
        ga, gb = own_faces(faces, pick_ref, w_ref, [ca, cb])
        tz, ta = product(split(z), w_ref[W_TIME]), product(ca, w_ref[W_TIME])
        out_ref[:elements, :] = (
            a + v_ref[:elements, :] - DAMPING * product(ca, w_ref[W_DIAG]) + sigma * (tz + ga)
        )
        out_ref[elements:, :] = (
            b + v_ref[elements:, :] - DAMPING * product(cb, w_ref[W_DIAG]) + sigma * (ta + gb)
        )

    (part4,) = call(
        third,
        [two],
        [re2, ro2, a3, b3, z3, v0, weights, pick, q_all, sigma_all],
        flops=2e9,
    )

    def last(re_ref, ro_ref, p_ref, w_ref, q_ref, sig_ref, out_ref):
        add = spread(q_ref[...], far_faces(faces, arrived(re_ref, ro_ref, slabs), w_ref), slabs)
        for t in range(slabs):
            out_ref[t * elements : (t + 1) * elements, :] = (
                p_ref[t * elements : (t + 1) * elements, :] + sig_ref[...] * add[t]
            )

    (out,) = call(
        last, [two], [re3, ro3, part4, weights, q_all, sigma_all], flops=1e7
    )
    return out.reshape(slabs, elements, width)


def solution(mesh):
    in_specs = (
        P("tm", "space", None),
        P("space"),
        P(),
        P(),
        P(),
        P(),
        P("space", None),
        P("space", None),
    )
    out_specs = P("tm", "space", None)
    return jax.shard_map(body, mesh=mesh, in_specs=in_specs, out_specs=out_specs, check_vma=False)
```

```python
import jax
import jax.numpy as jnp
from jax import lax
from jax.experimental import pallas as pl
from jax.experimental.pallas import tpu as pltpu
from jax.sharding import PartitionSpec as P

DAMPING = 0.7
F32 = jnp.float32
BF16 = jnp.bfloat16
VMEM = pltpu.VMEM
SMEM = pltpu.SMEM
HBM = pltpu.MemorySpace.HBM

W_DIAG, W_FACE, W_SOURCE_TIME, W_TIME = 0, 1, 5, 6


def call(kernel, out_shapes, args, spaces=None, scratch=(), flops=4e8):
    spaces = spaces or [VMEM] * len(args)
    args = [
        pltpu.with_memory_space_constraint(x, HBM) if s is HBM else x for x, s in zip(args, spaces)
    ]
    return pl.pallas_call(
        kernel,
        out_shape=[jax.ShapeDtypeStruct(s, d) for s, d in out_shapes],
        in_specs=[pl.BlockSpec(memory_space=s) for s in spaces],
        out_specs=[pl.BlockSpec(memory_space=VMEM)] * len(out_shapes),
        scratch_shapes=list(scratch),
        compiler_params=pltpu.CompilerParams(vmem_limit_bytes=24 << 20),
        cost_estimate=pl.CostEstimate(flops=int(flops), bytes_accessed=1 << 20, transcendentals=0),
    )(*args)


def fetch(pairs, sems):
    copies = [pltpu.make_async_copy(a, b, sems.at[i]) for i, (a, b) in enumerate(pairs)]
    for c in copies:
        c.start()
    return copies


def split(x):
    head = x.astype(BF16)
    tail = (x - head.astype(F32)).astype(BF16)
    return jnp.concatenate([head, tail], axis=1)


def halves(x):
    width = x.shape[1] // 2
    return x[:, :width] + x[:, width:]


def dot(left, right):
    return jnp.dot(left, right, preferred_element_type=F32)


def dot32(left, right):
    return jnp.dot(left, right, precision=lax.Precision.HIGHEST, preferred_element_type=F32)


def product(parts, tile):
    return halves(dot(parts, tile))


def weight_tile(w):
    head = w.astype(BF16)
    tail = (w - head.astype(F32)).astype(BF16)
    top = jnp.concatenate([head, tail], axis=1)
    low = jnp.concatenate([head, jnp.zeros_like(head)], axis=1)
    return jnp.concatenate([top, low], axis=0)


def column(row, width):
    return jnp.transpose(jnp.broadcast_to(row, (width, row.shape[1])))


def own_faces(faces, pick_ref, weights_ref, parts):
    count = len(parts)
    width = parts[0].shape[1]
    rows = parts[0].shape[0]
    every = jnp.concatenate(parts, axis=1) if count > 1 else parts[0]
    sums = [None] * count
    for face in range(faces):
        picked = dot(pick_ref[face * rows : (face + 1) * rows, :], every).astype(BF16)
        for i in range(count):
            term = dot(picked[:, i * width : (i + 1) * width], weights_ref[W_FACE + face])
            sums[i] = term if sums[i] is None else sums[i] + term
    return [halves(s) for s in sums]


def arrived(from_e, from_o, count):
    even = lax.axis_index("space") % 2 == 0
    left = jnp.where(even, from_o[...], from_e[...])
    right = jnp.where(even, from_e[...], from_o[...])
    rows = left.shape[0] // count
    return [
        jnp.concatenate([left[i * rows : (i + 1) * rows], right[i * rows : (i + 1) * rows]], axis=0)
        for i in range(count)
    ]


def far_faces(faces, rows_in, weights_ref):
    count = len(rows_in)
    n = rows_in[0].shape[0]
    parts = split(jnp.concatenate(rows_in, axis=0) if count > 1 else rows_in[0])
    per_face = [product(parts, weights_ref[W_FACE + f]) for f in range(faces)]
    lanes = [
        split(jnp.concatenate([u[i * n : (i + 1) * n] for u in per_face], axis=0))
        for i in range(count)
    ]
    return jnp.concatenate(lanes, axis=1) if count > 1 else lanes[0]


def spread(select, table, count):
    total = dot(select, table)
    width = total.shape[1] // count
    return [halves(total[:, i * width : (i + 1) * width]) for i in range(count)]


def put_sent(e_ref, o_ref, slabs):
    rows = slabs[0].shape[0] // 2
    for i, s in enumerate(slabs):
        e_ref[i * rows : (i + 1) * rows, :] = s[:rows]
        o_ref[i * rows : (i + 1) * rows, :] = s[rows:]


def at_sent(sent_ref, values):
    every = jnp.concatenate([split(v) for v in values], axis=1)
    return spread(sent_ref[...], every, len(values))


def body(
    source, elem_scale, diag_block, block_inverse, face_flux, time_trace, neighbours, send_rows
):
    slabs, elements, width = source.shape
    faces = neighbours.shape[1]
    sent = send_rows.shape[1]
    halo = sent // 2
    groups = lax.axis_size("tm")
    ring = lax.axis_size("space")
    flat = source.reshape(slabs * elements, width)
    scale_row = elem_scale.reshape(1, elements)
    faces_row = neighbours.T
    stack = W_TIME + groups - 1
    full = ((elements, width), F32)
    two = ((slabs * elements, width), F32)
    edge = ((slabs * halo, width), F32)
    far = faces * sent

    swap_e = [(i, i ^ 1) for i in range(ring)]
    swap_o = [(i, (i + 1) % ring if i % 2 else (i - 1) % ring) for i in range(ring)]

    def exchange(to_e, to_o):
        return lax.ppermute(to_e, "space", swap_e), lax.ppermute(to_o, "space", swap_o)

    def later(x, by):
        return lax.ppermute(x, "tm", [(i, (i + by) % groups) for i in range(groups)])

    def sent_at(send_ref, i):
        first = jnp.where(lax.axis_index("space") % 2 == 0, halo, 0)
        return send_ref[0, lax.rem(first + i, sent)]

    def first_kernel(
        s_hbm, scale_hbm, inv_hbm, send_hbm, e_ref, o_ref, xa_ref, xb_ref,
        s_ref, scale_ref, inv_ref, send_ref, g_ref, sems,
    ):
        copies = fetch(
            [(scale_hbm, scale_ref), (send_hbm, send_ref), (s_hbm, s_ref), (inv_hbm, inv_ref)],
            sems,
        )
        copies[0].wait()
        sigma = DAMPING / column(scale_ref[...], width)
        copies[1].wait()
        copies[2].wait()
        refs = [xa_ref, xb_ref]
        for t in range(slabs):
            refs[t][...] = s_ref[t * elements : (t + 1) * elements, :] * sigma
        for i in range(sent):
            at = sent_at(send_ref, i)
            base = (i // halo) * slabs * halo + i % halo
            for t in range(slabs):
                g_ref[base + t * halo : base + t * halo + 1, :] = refs[t][pl.ds(at, 1), :]
        copies[3].wait()
        out = dot32(g_ref[...], inv_ref[...])
        e_ref[...] = out[: slabs * halo]
        o_ref[...] = out[slabs * halo :]

    e0, o0, xa, xb = call(
        first_kernel,
        [edge, edge, full, full],
        [flat, scale_row, block_inverse, send_rows],
        spaces=[HBM] * 4,
        scratch=[
            VMEM((slabs * elements, width), F32),
            VMEM((1, elements), F32),
            VMEM((width, width), F32),
            SMEM((1, sent), jnp.int32),
            VMEM((slabs * sent, width), F32),
            pltpu.SemaphoreType.DMA((4,)),
        ],
        flops=1e7,
    )
    before = later(xb, 1)
    re0, ro0 = exchange(e0, o0)

    def setup_kernel(
        xa_ref, xb_ref, scale_hbm, d_hbm, inv_hbm, f_hbm, t_hbm, nbr_hbm, send_hbm,
        v_ref, part_ref, psent_ref, sigs_ref, w_ref, pick_ref, q_ref, qs_ref, sent_ref,
        sig_ref, frac_ref,
        scale_ref, d_ref, inv_ref, f_ref, t_ref, nbr_ref, send_ref, rows_ref, sems,
    ):
        copies = fetch(
            [
                (inv_hbm, inv_ref), (t_hbm, t_ref), (d_hbm, d_ref), (f_hbm, f_ref),
                (scale_hbm, scale_ref), (nbr_hbm, nbr_ref), (send_hbm, send_ref),
            ],
            sems,
        )
        for c in copies:
            c.wait()
        inv = inv_ref[...]
        trace = dot32(t_ref[...], inv)
        w_ref[W_DIAG] = weight_tile(dot32(d_ref[...], inv))
        for f in range(faces):
            w_ref[W_FACE + f] = weight_tile(dot32(f_ref[f], inv))
        w_ref[W_SOURCE_TIME] = weight_tile(dot32(inv, trace))
        power = trace
        for a in range(groups - 1):
            w_ref[W_TIME + a] = weight_tile(power)
            if a < groups - 2:
                power = dot32(power, trace)
        scale = column(scale_ref[...], width)
        sigma = DAMPING / scale
        sig_ref[...] = sigma
        frac_ref[...] = 1.0 / (2.0 * scale - 1.0)
        lane = lax.broadcasted_iota(jnp.int32, (elements, elements), 1)
        spot = lax.broadcasted_iota(jnp.int32, (elements, far), 1)
        wanted = jnp.zeros((elements, far), jnp.int32)
        for f in range(faces):
            wide = column(nbr_ref[f : f + 1, :], elements)
            pick_ref[f * elements : (f + 1) * elements, :] = jnp.where(
                wide == lane, 1.0, 0.0
            ).astype(BF16)
            wanted = jnp.where(spot // sent == f, column(nbr_ref[f : f + 1, :], far), wanted)
        q = jnp.where(wanted == elements + spot % sent, 1.0, 0.0).astype(BF16)
        q_ref[...] = q
        strip = lax.broadcasted_iota(jnp.int32, (1, elements), 1)
        for i in range(sent):
            rows_ref[i : i + 1, :] = jnp.where(strip == sent_at(send_ref, i), 1.0, 0.0)
        chosen = rows_ref[...].astype(BF16)
        sent_ref[...] = chosen
        qs_ref[...] = dot(chosen, q).astype(BF16)
        head = weight_tile(inv)
        v = [product(split(x[...]), head) for x in (xa_ref, xb_ref)]
        cut = [split(x) for x in v]
        near = own_faces(faces, pick_ref, w_ref, cut)
        parts = []
        for t in range(slabs):
            term = near[t]
            if t:
                term = term + product(cut[t - 1], w_ref[W_TIME])
            parts.append(
                2.0 * v[t] - DAMPING * product(cut[t], w_ref[W_DIAG]) + sigma * term
            )
            v_ref[t * elements : (t + 1) * elements, :] = v[t]
            part_ref[t * elements : (t + 1) * elements, :] = parts[t]
        got = at_sent(sent_ref, parts + [sigma])
        for t in range(slabs):
            psent_ref[t * sent : (t + 1) * sent, :] = got[t]
        sigs_ref[...] = got[slabs]

    (
        v0, part1, psent1, sig_sent, weights, pick, q_all, q_sent, choose, sigma_all, frac_all,
    ) = call(
        setup_kernel,
        [
            two, two, ((slabs * sent, width), F32), ((sent, width), F32),
            ((stack, 2 * width, 2 * width), BF16), ((faces * elements, elements), BF16),
            ((elements, far), BF16), ((sent, far), BF16), ((sent, elements), BF16), full, full,
        ],
        [
            xa, xb, scale_row, diag_block, block_inverse, face_flux, time_trace, faces_row,
            send_rows,
        ],
        spaces=[VMEM] * 2 + [HBM] * 7,
        scratch=[
            VMEM((1, elements), F32),
            VMEM((width, width), F32),
            VMEM((width, width), F32),
            VMEM((faces, width, width), F32),
            VMEM((width, width), F32),
            VMEM((faces, elements), jnp.int32),
            SMEM((1, sent), jnp.int32),
            VMEM((sent, elements), F32),
            pltpu.SemaphoreType.DMA((7,)),
        ],
        flops=2e9,
    )

    def time_mask(x, by=1):
        return jnp.where(lax.axis_index("tm") >= by, x, jnp.zeros_like(x))

    def edge_one(
        re_ref, ro_ref, b_ref, psent_ref, sigs_ref, w_ref, qs_ref, sent_ref, e_ref, o_ref
    ):
        table = far_faces(faces, arrived(re_ref, ro_ref, slabs), w_ref)
        add = spread(qs_ref[...], table, slabs)
        picked = dot(sent_ref[...], split(b_ref[...])).astype(BF16)
        old = time_mask(product(picked, w_ref[W_SOURCE_TIME]))
        sig = sigs_ref[...]
        new = [psent_ref[t * sent : (t + 1) * sent, :] + sig * add[t] for t in range(slabs)]
        new[0] = new[0] + sig * old
        put_sent(e_ref, o_ref, new)

    e1, o1 = call(
        edge_one,
        [edge, edge],
        [re0, ro0, before, psent1, sig_sent, weights, q_sent, choose],
        flops=1e7,
    )
    re1, ro1 = exchange(e1, o1)

    def middle(
        re_ref, ro_ref, b_ref, part_ref, v_ref, w_ref, pick_ref, q_ref, sig_ref, frac_ref,
        v1_ref, pa_ref, pb_ref, wp_ref, x_ref,
    ):
        sigma = sig_ref[...]
        frac = frac_ref[...]
        add = spread(q_ref[...], far_faces(faces, arrived(re_ref, ro_ref, slabs), w_ref), slabs)
        old = time_mask(product(split(b_ref[...]), w_ref[W_SOURCE_TIME]))
        va = part_ref[:elements, :] + sigma * add[0] + sigma * old
        vb = part_ref[elements:, :] + sigma * add[1]
        v0a, v0b = v_ref[:elements, :], v_ref[elements:, :]
        v1_ref[...] = vb
        ca, cb = split(va), split(vb)
        ga, gb = own_faces(faces, pick_ref, w_ref, [ca, cb])
        da, db = product(ca, w_ref[W_DIAG]), product(cb, w_ref[W_DIAG])
        ta, tb = product(ca, w_ref[W_TIME]), product(cb, w_ref[W_TIME])
        pa_ref[...] = va + v0a - DAMPING * da + sigma * ga
        pb_ref[...] = vb + v0b - DAMPING * db + sigma * (ta + gb)
        wp_ref[...] = (
            frac * (((v0a + v0b) - DAMPING * (da + db)) / sigma + ta + ga + gb) + vb
        )
        x_ref[...] = v0b + sigma * (ta - tb)

    v1b, pa0, pb0, wp, x_own = call(
        middle,
        [full] * 5,
        [re0, ro0, before, part1, v0, weights, pick, q_all, sigma_all, frac_all],
        flops=2e9,
    )

    def coarse_kernel(
        re_ref, ro_ref, wp_ref, pa_ref, pb_ref, w_ref, q_ref, sig_ref, frac_ref,
        w_out, pa_out, pb_out,
    ):
        add = spread(q_ref[...], far_faces(faces, arrived(re_ref, ro_ref, slabs), w_ref), slabs)
        w_out[...] = wp_ref[...] + frac_ref[...] * (add[0] + add[1])
        pa_out[...] = pa_ref[...] + sig_ref[...] * add[0]
        pb_out[...] = pb_ref[...] + sig_ref[...] * add[1]

    w_own, pa1, pb1 = call(
        coarse_kernel,
        [full] * 3,
        [re1, ro1, wp, pa0, pb0, weights, q_all, sigma_all, frac_all],
        flops=1e7,
    )
    earlier = [later(w_own, a) for a in range(1, groups)]
    x_before = later(x_own, 1)

    def recur(*refs):
        olds = refs[: groups - 1]
        w_own_ref, v1_ref, w_ref, sent_ref, frac_ref, c_ref, d_ref, e_ref, o_ref = refs[
            groups - 1 :
        ]
        frac = frac_ref[...]
        d = time_mask(olds[0][...])
        c = w_own_ref[...] - v1_ref[...]
        power = frac
        for a in range(1, groups):
            cut = split(time_mask(power * olds[a - 1][...], a))
            c = c + product(cut, w_ref[W_TIME + a - 1])
            if a < groups - 1:
                cut = split(time_mask(power * olds[a][...], a + 1))
                d = d + product(cut, w_ref[W_TIME + a - 1])
                power = power * frac
        c_ref[...] = c
        d_ref[...] = d
        put_sent(e_ref, o_ref, at_sent(sent_ref, [c, d]))

    c_all, d_all, e2, o2 = call(
        recur,
        [full, full, edge, edge],
        [*earlier, w_own, v1b, weights, choose, frac_all],
        flops=1e8,
    )
    re2, ro2 = exchange(e2, o2)

    def second(
        c_in, d_in, xb_ref, pa_ref, pb_ref, w_ref, pick_ref, sig_ref, sent_ref,
        a_ref, b_ref, z_ref, ps_ref,
    ):
        sigma = sig_ref[...]
        c, d = c_in[...], d_in[...]
        cc, cd = split(c), split(d)
        gc, gd = own_faces(faces, pick_ref, w_ref, [cc, cd])
        same = c - DAMPING * product(cc, w_ref[W_DIAG]) + sigma * gc
        td = product(cd, w_ref[W_TIME])
        a = pa_ref[...] + same + sigma * td
        b = pb_ref[...] + same + sigma * product(cc, w_ref[W_TIME])
        a_ref[...] = a
        b_ref[...] = b
        z_ref[...] = (
            time_mask(xb_ref[...]) + d - DAMPING * product(cd, w_ref[W_DIAG]) + sigma * (td + gd)
        )
        got = at_sent(sent_ref, [a, b])
        for t in range(slabs):
            ps_ref[t * sent : (t + 1) * sent, :] = got[t]

    a3, b3, z3, psent3 = call(
        second,
        [full, full, full, ((slabs * sent, width), F32)],
        [c_all, d_all, x_before, pa1, pb1, weights, pick, sigma_all, choose],
        flops=2e9,
    )

    def edge_two(re_ref, ro_ref, psent_ref, sigs_ref, w_ref, qs_ref, e_ref, o_ref):
        table = far_faces(faces, arrived(re_ref, ro_ref, 2)[:1], w_ref)
        add = sigs_ref[...] * spread(qs_ref[...], table, 1)[0]
        put_sent(
            e_ref, o_ref, [psent_ref[t * sent : (t + 1) * sent, :] + add for t in range(slabs)]
        )

    e3, o3 = call(
        edge_two,
        [edge, edge],
        [re2, ro2, psent3, sig_sent, weights, q_sent],
        flops=1e7,
    )
    re3, ro3 = exchange(e3, o3)

    def third(
        re_ref, ro_ref, a_in, b_in, z_in, v_ref, w_ref, pick_ref, q_ref, sig_ref, out_ref
    ):
        sigma = sig_ref[...]
        add = spread(q_ref[...], far_faces(faces, arrived(re_ref, ro_ref, 2), w_ref), 2)
        a = a_in[...] + sigma * add[0]
        b = b_in[...] + sigma * add[0]
        z = z_in[...] + sigma * add[1]
        ca, cb = split(a), split(b)
        ga, gb = own_faces(faces, pick_ref, w_ref, [ca, cb])
        tz, ta = product(split(z), w_ref[W_TIME]), product(ca, w_ref[W_TIME])
        out_ref[:elements, :] = (
            a + v_ref[:elements, :] - DAMPING * product(ca, w_ref[W_DIAG]) + sigma * (tz + ga)
        )
        out_ref[elements:, :] = (
            b + v_ref[elements:, :] - DAMPING * product(cb, w_ref[W_DIAG]) + sigma * (ta + gb)
        )

    (part4,) = call(
        third,
        [two],
        [re2, ro2, a3, b3, z3, v0, weights, pick, q_all, sigma_all],
        flops=2e9,
    )

    def last(re_ref, ro_ref, p_ref, w_ref, q_ref, sig_ref, out_ref):
        add = spread(q_ref[...], far_faces(faces, arrived(re_ref, ro_ref, slabs), w_ref), slabs)
        for t in range(slabs):
            out_ref[t * elements : (t + 1) * elements, :] = (
                p_ref[t * elements : (t + 1) * elements, :] + sig_ref[...] * add[t]
            )

    (out,) = call(
        last, [two], [re3, ro3, part4, weights, q_all, sigma_all], flops=1e7
    )
    return out.reshape(slabs, elements, width)


def solution(mesh):
    in_specs = (
        P("tm", "space", None),
        P("space"),
        P(),
        P(),
        P(),
        P(),
        P("space", None),
        P("space", None),
    )
    out_specs = P("tm", "space", None)
    return jax.shard_map(body, mesh=mesh, in_specs=in_specs, out_specs=out_specs, check_vma=False)
```

```python
import jax
import jax.numpy as jnp
from jax import lax
from jax.experimental import pallas as pl
from jax.experimental.pallas import tpu as pltpu
from jax.sharding import PartitionSpec as P

DAMPING = 0.7
F32 = jnp.float32
BF16 = jnp.bfloat16
VMEM = pltpu.VMEM
SMEM = pltpu.SMEM
HBM = pltpu.MemorySpace.HBM

W_DIAG, W_FACE, W_SOURCE_TIME, W_TIME = 0, 1, 5, 6


def call(kernel, out_shapes, args, spaces=None, scratch=(), flops=4e8):
    spaces = spaces or [VMEM] * len(args)
    args = [
        pltpu.with_memory_space_constraint(x, HBM) if s is HBM else x for x, s in zip(args, spaces)
    ]
    return pl.pallas_call(
        kernel,
        out_shape=[jax.ShapeDtypeStruct(s, d) for s, d in out_shapes],
        in_specs=[pl.BlockSpec(memory_space=s) for s in spaces],
        out_specs=[pl.BlockSpec(memory_space=VMEM)] * len(out_shapes),
        scratch_shapes=list(scratch),
        compiler_params=pltpu.CompilerParams(vmem_limit_bytes=24 << 20),
        cost_estimate=pl.CostEstimate(flops=int(flops), bytes_accessed=1 << 20, transcendentals=0),
    )(*args)


def fetch(pairs, sems):
    copies = [pltpu.make_async_copy(a, b, sems.at[i]) for i, (a, b) in enumerate(pairs)]
    for c in copies:
        c.start()
    return copies


def split(x):
    head = x.astype(BF16)
    tail = (x - head.astype(F32)).astype(BF16)
    return jnp.concatenate([head, tail], axis=1)


def halves(x):
    width = x.shape[1] // 2
    return x[:, :width] + x[:, width:]


def dot(left, right):
    return jnp.dot(left, right, preferred_element_type=F32)


def dot32(left, right):
    return jnp.dot(left, right, precision=lax.Precision.HIGHEST, preferred_element_type=F32)


def product(parts, tile):
    return halves(dot(parts, tile))


def weight_tile(w):
    head = w.astype(BF16)
    tail = (w - head.astype(F32)).astype(BF16)
    top = jnp.concatenate([head, tail], axis=1)
    low = jnp.concatenate([head, jnp.zeros_like(head)], axis=1)
    return jnp.concatenate([top, low], axis=0)


def column(row, width):
    return jnp.transpose(jnp.broadcast_to(row, (width, row.shape[1])))


def own_faces(faces, pick_ref, weights_ref, parts):
    count = len(parts)
    width = parts[0].shape[1]
    rows = parts[0].shape[0]
    every = jnp.concatenate(parts, axis=1) if count > 1 else parts[0]
    sums = [None] * count
    for face in range(faces):
        picked = dot(pick_ref[face * rows : (face + 1) * rows, :], every).astype(BF16)
        for i in range(count):
            term = dot(picked[:, i * width : (i + 1) * width], weights_ref[W_FACE + face])
            sums[i] = term if sums[i] is None else sums[i] + term
    return [halves(s) for s in sums]


def arrived(from_e, from_o, count):
    even = lax.axis_index("space") % 2 == 0
    left = jnp.where(even, from_o[...], from_e[...])
    right = jnp.where(even, from_e[...], from_o[...])
    rows = left.shape[0] // count
    return [
        jnp.concatenate([left[i * rows : (i + 1) * rows], right[i * rows : (i + 1) * rows]], axis=0)
        for i in range(count)
    ]


def far_faces(faces, rows_in, weights_ref):
    count = len(rows_in)
    n = rows_in[0].shape[0]
    parts = split(jnp.concatenate(rows_in, axis=0) if count > 1 else rows_in[0])
    per_face = [product(parts, weights_ref[W_FACE + f]) for f in range(faces)]
    lanes = [
        split(jnp.concatenate([u[i * n : (i + 1) * n] for u in per_face], axis=0))
        for i in range(count)
    ]
    return jnp.concatenate(lanes, axis=1) if count > 1 else lanes[0]


def spread(select, table, count):
    total = dot(select, table)
    width = total.shape[1] // count
    return [halves(total[:, i * width : (i + 1) * width]) for i in range(count)]


def put_sent(e_ref, o_ref, slabs):
    rows = slabs[0].shape[0] // 2
    for i, s in enumerate(slabs):
        e_ref[i * rows : (i + 1) * rows, :] = s[:rows]
        o_ref[i * rows : (i + 1) * rows, :] = s[rows:]


def at_sent(sent_ref, values):
    every = jnp.concatenate([split(v) for v in values], axis=1)
    return spread(sent_ref[...], every, len(values))


def body(
    source, elem_scale, diag_block, block_inverse, face_flux, time_trace, neighbours, send_rows
):
    slabs, elements, width = source.shape
    faces = neighbours.shape[1]
    sent = send_rows.shape[1]
    halo = sent // 2
    groups = lax.axis_size("tm")
    ring = lax.axis_size("space")
    flat = source.reshape(slabs * elements, width)
    scale_row = elem_scale.reshape(1, elements)
    faces_row = neighbours.T
    stack = W_TIME + groups - 1
    full = ((elements, width), F32)
    two = ((slabs * elements, width), F32)
    edge = ((slabs * halo, width), F32)
    far = faces * sent

    swap_e = [(i, i ^ 1) for i in range(ring)]
    swap_o = [(i, (i + 1) % ring if i % 2 else (i - 1) % ring) for i in range(ring)]

    def over_e(x):
        return lax.ppermute(x, "space", swap_e)

    def over_o(x):
        return lax.ppermute(x, "space", swap_o)

    def later(x, by):
        return lax.ppermute(x, "tm", [(i, (i + by) % groups) for i in range(groups)])

    def sent_at(send_ref, i):
        first = jnp.where(lax.axis_index("space") % 2 == 0, halo, 0)
        return send_ref[0, lax.rem(first + i, sent)]

    def first_kernel(
        s_hbm, scale_hbm, inv_hbm, send_hbm, e_ref, o_ref, xa_ref, xb_ref,
        s_ref, scale_ref, inv_ref, send_ref, g_ref, sems,
    ):
        copies = fetch(
            [(scale_hbm, scale_ref), (send_hbm, send_ref), (s_hbm, s_ref), (inv_hbm, inv_ref)],
            sems,
        )
        copies[0].wait()
        sigma = DAMPING / column(scale_ref[...], width)
        copies[1].wait()
        copies[2].wait()
        refs = [xa_ref, xb_ref]
        for t in range(slabs):
            refs[t][...] = s_ref[t * elements : (t + 1) * elements, :] * sigma
        for i in range(sent):
            at = sent_at(send_ref, i)
            base = (i // halo) * slabs * halo + i % halo
            for t in range(slabs):
                g_ref[base + t * halo : base + t * halo + 1, :] = refs[t][pl.ds(at, 1), :]
        copies[3].wait()
        out = dot32(g_ref[...], inv_ref[...])
        e_ref[...] = out[: slabs * halo]
        o_ref[...] = out[slabs * halo :]

    e0, o0, xa, xb = call(
        first_kernel,
        [edge, edge, full, full],
        [flat, scale_row, block_inverse, send_rows],
        spaces=[HBM] * 4,
        scratch=[
            VMEM((slabs * elements, width), F32),
            VMEM((1, elements), F32),
            VMEM((width, width), F32),
            SMEM((1, sent), jnp.int32),
            VMEM((slabs * sent, width), F32),
            pltpu.SemaphoreType.DMA((4,)),
        ],
        flops=1e7,
    )
    before = later(xb, 1)
    re0, ro0 = over_e(e0), over_o(o0)

    def setup_kernel(
        xa_ref, xb_ref, scale_hbm, d_hbm, inv_hbm, f_hbm, t_hbm, nbr_hbm, send_hbm,
        v_ref, part_ref, psent_ref, sigs_ref, fracs_ref, w_ref, pick_ref, picko_ref, q_ref, qs_ref,
        qo_ref, sent_ref, sig_ref, frac_ref,
        scale_ref, d_ref, inv_ref, f_ref, t_ref, nbr_ref, send_ref, rows_ref, sems,
    ):
        copies = fetch(
            [
                (inv_hbm, inv_ref), (t_hbm, t_ref), (d_hbm, d_ref), (f_hbm, f_ref),
                (scale_hbm, scale_ref), (nbr_hbm, nbr_ref), (send_hbm, send_ref),
            ],
            sems,
        )
        for c in copies:
            c.wait()
        inv = inv_ref[...]
        trace = dot32(t_ref[...], inv)
        w_ref[W_DIAG] = weight_tile(dot32(d_ref[...], inv))
        for f in range(faces):
            w_ref[W_FACE + f] = weight_tile(dot32(f_ref[f], inv))
        w_ref[W_SOURCE_TIME] = weight_tile(dot32(inv, trace))
        power = trace
        for a in range(groups - 1):
            w_ref[W_TIME + a] = weight_tile(power)
            if a < groups - 2:
                power = dot32(power, trace)
        scale = column(scale_ref[...], width)
        sigma = DAMPING / scale
        sig_ref[...] = sigma
        frac = 1.0 / (2.0 * scale - 1.0)
        frac_ref[...] = frac
        lane = lax.broadcasted_iota(jnp.int32, (elements, elements), 1)
        spot = lax.broadcasted_iota(jnp.int32, (elements, far), 1)
        wanted = jnp.zeros((elements, far), jnp.int32)
        for f in range(faces):
            wide = column(nbr_ref[f : f + 1, :], elements)
            pick_ref[f * elements : (f + 1) * elements, :] = jnp.where(
                wide == lane, 1.0, 0.0
            ).astype(BF16)
            wanted = jnp.where(spot // sent == f, column(nbr_ref[f : f + 1, :], far), wanted)
        q = jnp.where(wanted == elements + spot % sent, 1.0, 0.0).astype(BF16)
        q_ref[...] = q
        strip = lax.broadcasted_iota(jnp.int32, (1, elements), 1)
        for i in range(sent):
            rows_ref[i : i + 1, :] = jnp.where(strip == sent_at(send_ref, i), 1.0, 0.0)
        chosen = rows_ref[...].astype(BF16)
        sent_ref[...] = chosen
        qs = dot(chosen, q)
        qs_ref[...] = qs.astype(BF16)
        for f in range(faces):
            picko_ref[f * halo : (f + 1) * halo, :] = dot(
                chosen[halo:], pick_ref[f * elements : (f + 1) * elements, :]
            ).astype(BF16)
        head = weight_tile(inv)
        v = [product(split(x[...]), head) for x in (xa_ref, xb_ref)]
        cut = [split(x) for x in v]
        near = own_faces(faces, pick_ref, w_ref, cut)
        parts = []
        for t in range(slabs):
            term = near[t]
            if t:
                term = term + product(cut[t - 1], w_ref[W_TIME])
            parts.append(
                2.0 * v[t] - DAMPING * product(cut[t], w_ref[W_DIAG]) + sigma * term
            )
            v_ref[t * elements : (t + 1) * elements, :] = v[t]
            part_ref[t * elements : (t + 1) * elements, :] = parts[t]
        got = at_sent(sent_ref, parts + [sigma, frac])
        for t in range(slabs):
            psent_ref[t * sent : (t + 1) * sent, :] = got[t]
        sigs_ref[...] = got[slabs]
        fracs_ref[...] = got[slabs + 1]
        near_half = lax.broadcasted_iota(jnp.int32, (halo, far), 1) % sent < halo
        even = lax.axis_index("space") % 2 == 0
        kept = jnp.where(near_half, jnp.where(even, 1.0, 0.0), jnp.where(even, 0.0, 1.0))
        qo_ref[...] = got[slabs + 1][halo:] * qs[halo:] * kept

    (
        v0, part1, psent1, sig_sent, frac_sent, weights, pick, pick_o, q_all, q_sent, q_o, choose,
        sigma_all, frac_all,
    ) = call(
        setup_kernel,
        [
            two, two, ((slabs * sent, width), F32), ((sent, width), F32), ((sent, width), F32),
            ((stack, 2 * width, 2 * width), BF16), ((faces * elements, elements), BF16),
            ((faces * halo, elements), BF16), ((elements, far), BF16), ((sent, far), BF16),
            ((halo, far), F32), ((sent, elements), BF16), full, full,
        ],
        [
            xa, xb, scale_row, diag_block, block_inverse, face_flux, time_trace, faces_row,
            send_rows,
        ],
        spaces=[VMEM] * 2 + [HBM] * 7,
        scratch=[
            VMEM((1, elements), F32),
            VMEM((width, width), F32),
            VMEM((width, width), F32),
            VMEM((faces, width, width), F32),
            VMEM((width, width), F32),
            VMEM((faces, elements), jnp.int32),
            SMEM((1, sent), jnp.int32),
            VMEM((sent, elements), F32),
            pltpu.SemaphoreType.DMA((7,)),
        ],
        flops=2e9,
    )

    def time_mask(x, by=1):
        return jnp.where(lax.axis_index("tm") >= by, x, jnp.zeros_like(x))

    def edge_one(
        re_ref, ro_ref, b_ref, psent_ref, sigs_ref, w_ref, qs_ref, sent_ref, e_ref, o_ref
    ):
        table = far_faces(faces, arrived(re_ref, ro_ref, slabs), w_ref)
        add = spread(qs_ref[...], table, slabs)
        picked = dot(sent_ref[...], split(b_ref[...])).astype(BF16)
        old = time_mask(product(picked, w_ref[W_SOURCE_TIME]))
        sig = sigs_ref[...]
        new = [psent_ref[t * sent : (t + 1) * sent, :] + sig * add[t] for t in range(slabs)]
        new[0] = new[0] + sig * old
        put_sent(e_ref, o_ref, new)

    e1, vo = call(
        edge_one,
        [edge, edge],
        [re0, ro0, before, psent1, sig_sent, weights, q_sent, choose],
        flops=1e7,
    )
    re1 = over_e(e1)

    def ahead(
        re_ref, ro_ref, b_ref, part_ref, vo_ref, o0_ref, w_ref, picko_ref, q_ref, sig_ref,
        sigs_ref, fracs_ref, v1_ref, wo_ref,
    ):
        sigma = sig_ref[...]
        add = spread(q_ref[...], far_faces(faces, arrived(re_ref, ro_ref, slabs), w_ref), slabs)
        old = time_mask(product(split(b_ref[...]), w_ref[W_SOURCE_TIME]))
        va = part_ref[:elements, :] + sigma * add[0] + sigma * old
        vb = part_ref[elements:, :] + sigma * add[1]
        v1_ref[:elements, :] = va
        v1_ref[elements:, :] = vb
        picked = dot(picko_ref[...], split(va + vb)).astype(BF16)
        near = None
        for f in range(faces):
            term = dot(picked[f * halo : (f + 1) * halo], w_ref[W_FACE + f])
            near = term if near is None else near + term
        sa, sb = vo_ref[:halo, :], vo_ref[halo:, :]
        rest = (
            o0_ref[:halo, :] + o0_ref[halo:, :] - DAMPING * product(split(sa + sb), w_ref[W_DIAG])
        ) / sigs_ref[halo:, :]
        rest = rest + product(split(sa), w_ref[W_TIME]) + halves(near)
        wo_ref[...] = fracs_ref[halo:, :] * rest + sb

    v1, w_part = call(
        ahead,
        [two, ((halo, width), F32)],
        [
            re0, ro0, before, part1, vo, o0, weights, pick_o, q_all, sigma_all, sig_sent,
            frac_sent,
        ],
        flops=2e8,
    )

    def edge_w(re_ref, wo_ref, vo_ref, w_ref, qs_ref, fracs_ref, qo_ref, o_ref):
        both = re_ref[:halo, :] + re_ref[halo:, :]
        none = jnp.zeros_like(both)
        even = lax.axis_index("space") % 2 == 0
        rows = jnp.concatenate([jnp.where(even, none, both), jnp.where(even, both, none)], axis=0)
        add = spread(qs_ref[halo:, :], far_faces(faces, [rows], w_ref), 1)[0]
        frac = fracs_ref[halo:, :]
        o_ref[: slabs * halo, :] = vo_ref[...]
        o_ref[slabs * halo : (slabs + 1) * halo, :] = wo_ref[...] + frac * add
        o_ref[(slabs + 1) * halo : (slabs + 2) * halo, :] = qo_ref[...]
        o_ref[(slabs + 2) * halo :, :] = frac

    (o1,) = call(
        edge_w,
        [(((slabs + 3) * halo, width), F32)],
        [re1, w_part, vo, weights, q_sent, frac_sent, q_o],
        flops=1e7,
    )
    ro1 = over_o(o1)

    def middle(
        v1_ref, v_ref, w_ref, pick_ref, sig_ref, frac_ref, pa_ref, pb_ref, wp_ref, x_ref
    ):
        sigma = sig_ref[...]
        frac = frac_ref[...]
        va, vb = v1_ref[:elements, :], v1_ref[elements:, :]
        v0a, v0b = v_ref[:elements, :], v_ref[elements:, :]
        ca, cb = split(va), split(vb)
        ga, gb = own_faces(faces, pick_ref, w_ref, [ca, cb])
        da, db = product(ca, w_ref[W_DIAG]), product(cb, w_ref[W_DIAG])
        ta, tb = product(ca, w_ref[W_TIME]), product(cb, w_ref[W_TIME])
        pa_ref[...] = va + v0a - DAMPING * da + sigma * ga
        pb_ref[...] = vb + v0b - DAMPING * db + sigma * (ta + gb)
        wp_ref[...] = (
            frac * (((v0a + v0b) - DAMPING * (da + db)) / sigma + ta + ga + gb) + vb
        )
        x_ref[...] = v0b + sigma * (ta - tb)

    pa0, pb0, wp, x_own = call(
        middle,
        [full] * 4,
        [v1, v0, weights, pick, sigma_all, frac_all],
        flops=1e9,
    )

    more = ((elements + halo, width), F32)

    def coarse_kernel(
        re_ref, ro_ref, vo_ref, wp_ref, pa_ref, pb_ref, w_ref, q_ref, sig_ref, frac_ref,
        w_out, pa_out, pb_out,
    ):
        rows = arrived(re_ref, ro_ref.at[: slabs * halo, :], slabs)
        both = vo_ref[:halo, :] + vo_ref[halo:, :]
        rows.append(jnp.concatenate([both, both], axis=0))
        table = far_faces(faces, rows, w_ref)
        lanes = 2 * width
        add = spread(q_ref[...], table[:, : slabs * lanes], slabs)
        mine = halves(table[:, slabs * lanes :].astype(F32))
        w_out[:elements, :] = wp_ref[...] + frac_ref[...] * (add[0] + add[1])
        w_out[elements:, :] = ro_ref[slabs * halo : (slabs + 1) * halo, :] + dot32(
            ro_ref[(slabs + 1) * halo : (slabs + 2) * halo, :], mine
        )
        pa_out[...] = pa_ref[...] + sig_ref[...] * add[0]
        pb_out[...] = pb_ref[...] + sig_ref[...] * add[1]

    w_own, pa1, pb1 = call(
        coarse_kernel,
        [more, full, full],
        [re1, ro1, vo, wp, pa0, pb0, weights, q_all, sigma_all, frac_all],
        flops=1e7,
    )
    earlier = [later(w_own, a) for a in range(1, groups)]
    x_before = later(x_own, 1)

    def recur(*refs):
        olds = refs[: groups - 1]
        w_own_ref, v1_ref, ro_ref, w_ref, sent_ref, frac_ref, c_ref, d_ref, e_ref, oh_ref = refs[
            groups - 1 :
        ]
        frac = jnp.concatenate([frac_ref[...], ro_ref[(slabs + 2) * halo :, :]], axis=0)
        v_last = jnp.concatenate(
            [v1_ref[(slabs - 1) * elements :, :], ro_ref[(slabs - 1) * halo : slabs * halo, :]],
            axis=0,
        )
        d = time_mask(olds[0][...])
        c = w_own_ref[...] - v_last
        power = frac
        for a in range(1, groups):
            cut = split(time_mask(power * olds[a - 1][...], a))
            c = c + product(cut, w_ref[W_TIME + a - 1])
            if a < groups - 1:
                cut = split(time_mask(power * olds[a][...], a + 1))
                d = d + product(cut, w_ref[W_TIME + a - 1])
                power = power * frac
        c_ref[...] = c[:elements]
        d_ref[...] = d[:elements]
        oh_ref[:halo, :] = c[elements:]
        oh_ref[halo:, :] = d[elements:]
        every = jnp.concatenate([split(c[:elements]), split(d[:elements])], axis=1)
        got = spread(sent_ref[:halo, :], every, 2)
        e_ref[:halo, :] = got[0]
        e_ref[halo:, :] = got[1]

    c_all, d_all, e2, ro2 = call(
        recur,
        [full, full, edge, edge],
        [*earlier, w_own, v1, ro1, weights, choose, frac_all],
        flops=1e8,
    )
    re2 = over_e(e2)

    def second(
        c_in, d_in, xb_ref, pa_ref, pb_ref, w_ref, pick_ref, sig_ref, sent_ref,
        a_ref, b_ref, z_ref, ps_ref,
    ):
        sigma = sig_ref[...]
        c, d = c_in[...], d_in[...]
        cc, cd = split(c), split(d)
        gc, gd = own_faces(faces, pick_ref, w_ref, [cc, cd])
        same = c - DAMPING * product(cc, w_ref[W_DIAG]) + sigma * gc
        td = product(cd, w_ref[W_TIME])
        a = pa_ref[...] + same + sigma * td
        b = pb_ref[...] + same + sigma * product(cc, w_ref[W_TIME])
        a_ref[...] = a
        b_ref[...] = b
        z_ref[...] = (
            time_mask(xb_ref[...]) + d - DAMPING * product(cd, w_ref[W_DIAG]) + sigma * (td + gd)
        )
        got = at_sent(sent_ref, [a, b])
        for t in range(slabs):
            ps_ref[t * sent : (t + 1) * sent, :] = got[t]

    a3, b3, z3, psent3 = call(
        second,
        [full, full, full, ((slabs * sent, width), F32)],
        [c_all, d_all, x_before, pa1, pb1, weights, pick, sigma_all, choose],
        flops=2e9,
    )

    def edge_two(re_ref, ro_ref, psent_ref, sigs_ref, w_ref, qs_ref, e_ref, o_ref):
        table = far_faces(faces, arrived(re_ref, ro_ref, 2)[:1], w_ref)
        add = sigs_ref[...] * spread(qs_ref[...], table, 1)[0]
        put_sent(
            e_ref, o_ref, [psent_ref[t * sent : (t + 1) * sent, :] + add for t in range(slabs)]
        )

    e3, o3 = call(
        edge_two,
        [edge, edge],
        [re2, ro2, psent3, sig_sent, weights, q_sent],
        flops=1e7,
    )
    re3, ro3 = over_e(e3), over_o(o3)

    def third(
        re_ref, ro_ref, a_in, b_in, z_in, v_ref, w_ref, pick_ref, q_ref, sig_ref, out_ref
    ):
        sigma = sig_ref[...]
        add = spread(q_ref[...], far_faces(faces, arrived(re_ref, ro_ref, 2), w_ref), 2)
        a = a_in[...] + sigma * add[0]
        b = b_in[...] + sigma * add[0]
        z = z_in[...] + sigma * add[1]
        ca, cb = split(a), split(b)
        ga, gb = own_faces(faces, pick_ref, w_ref, [ca, cb])
        tz, ta = product(split(z), w_ref[W_TIME]), product(ca, w_ref[W_TIME])
        out_ref[:elements, :] = (
            a + v_ref[:elements, :] - DAMPING * product(ca, w_ref[W_DIAG]) + sigma * (tz + ga)
        )
        out_ref[elements:, :] = (
            b + v_ref[elements:, :] - DAMPING * product(cb, w_ref[W_DIAG]) + sigma * (ta + gb)
        )

    (part4,) = call(
        third,
        [two],
        [re2, ro2, a3, b3, z3, v0, weights, pick, q_all, sigma_all],
        flops=2e9,
    )

    def last(re_ref, ro_ref, p_ref, w_ref, q_ref, sig_ref, out_ref):
        add = spread(q_ref[...], far_faces(faces, arrived(re_ref, ro_ref, slabs), w_ref), slabs)
        for t in range(slabs):
            out_ref[t * elements : (t + 1) * elements, :] = (
                p_ref[t * elements : (t + 1) * elements, :] + sig_ref[...] * add[t]
            )

    (out,) = call(
        last, [two], [re3, ro3, part4, weights, q_all, sigma_all], flops=1e7
    )
    return out.reshape(slabs, elements, width)


def solution(mesh):
    in_specs = (
        P("tm", "space", None),
        P("space"),
        P(),
        P(),
        P(),
        P(),
        P("space", None),
        P("space", None),
    )
    out_specs = P("tm", "space", None)
    return jax.shard_map(body, mesh=mesh, in_specs=in_specs, out_specs=out_specs, check_vma=False)
```

```python
import jax
import jax.numpy as jnp
from jax import lax
from jax.experimental import pallas as pl
from jax.experimental.pallas import tpu as pltpu
from jax.sharding import PartitionSpec as P


DAMPING = 0.7
F32 = jnp.float32
BF16 = jnp.bfloat16
VMEM = pltpu.VMEM
SMEM = pltpu.SMEM
HBM = pltpu.MemorySpace.HBM

W_DIAG, W_FACE, W_SOURCE_TIME, W_TIME = 0, 1, 5, 6


def call(kernel, out_shapes, args, spaces=None, scratch=(), flops=4e8, out_space=VMEM):
    spaces = spaces or [VMEM] * len(args)
    args = [
        pltpu.with_memory_space_constraint(x, HBM) if s is HBM else x for x, s in zip(args, spaces)
    ]
    return pl.pallas_call(
        kernel,
        out_shape=[jax.ShapeDtypeStruct(s, d) for s, d in out_shapes],
        in_specs=[pl.BlockSpec(memory_space=s) for s in spaces],
        out_specs=[pl.BlockSpec(memory_space=out_space)] * len(out_shapes),
        scratch_shapes=list(scratch),
        compiler_params=pltpu.CompilerParams(vmem_limit_bytes=24 << 20),
        cost_estimate=pl.CostEstimate(flops=int(flops), bytes_accessed=1 << 20, transcendentals=0),
    )(*args)


def fetch(pairs, sems):
    copies = [pltpu.make_async_copy(a, b, sems.at[i]) for i, (a, b) in enumerate(pairs)]
    for c in copies:
        c.start()
    return copies


def split(x):
    head = x.astype(BF16)
    tail = (x - head.astype(F32)).astype(BF16)
    return jnp.concatenate([head, tail], axis=1)


def halves(x):
    width = x.shape[1] // 2
    return x[:, :width] + x[:, width:]


def dot(left, right):
    return jnp.dot(left, right, preferred_element_type=F32)


def dot32(left, right):
    return jnp.dot(left, right, precision=lax.Precision.HIGHEST, preferred_element_type=F32)


def product(parts, tile):
    return halves(dot(parts, tile))


def weight_tile(w):
    head = w.astype(BF16)
    tail = (w - head.astype(F32)).astype(BF16)
    top = jnp.concatenate([head, tail], axis=1)
    low = jnp.concatenate([head, jnp.zeros_like(head)], axis=1)
    return jnp.concatenate([top, low], axis=0)


def column(row, width):
    return jnp.transpose(jnp.broadcast_to(row, (width, row.shape[1])))


def own_faces(faces, pick_ref, weights_ref, parts):
    count = len(parts)
    width = parts[0].shape[1]
    rows = parts[0].shape[0]
    every = jnp.concatenate(parts, axis=1) if count > 1 else parts[0]
    sums = [None] * count
    for face in range(faces):
        picked = dot(pick_ref[face * rows : (face + 1) * rows, :], every).astype(BF16)
        for i in range(count):
            term = dot(picked[:, i * width : (i + 1) * width], weights_ref[W_FACE + face])
            sums[i] = term if sums[i] is None else sums[i] + term
    return [halves(s) for s in sums]


def arrived(from_e, from_o, count):
    even = lax.axis_index("space") % 2 == 0
    left = jnp.where(even, from_o[...], from_e[...])
    right = jnp.where(even, from_e[...], from_o[...])
    rows = left.shape[0] // count
    return [
        jnp.concatenate([left[i * rows : (i + 1) * rows], right[i * rows : (i + 1) * rows]], axis=0)
        for i in range(count)
    ]


def far_faces(faces, rows_in, weights_ref):
    count = len(rows_in)
    n = rows_in[0].shape[0]
    parts = split(jnp.concatenate(rows_in, axis=0) if count > 1 else rows_in[0])
    per_face = [product(parts, weights_ref[W_FACE + f]) for f in range(faces)]
    lanes = [
        split(jnp.concatenate([u[i * n : (i + 1) * n] for u in per_face], axis=0))
        for i in range(count)
    ]
    return jnp.concatenate(lanes, axis=1) if count > 1 else lanes[0]


def spread(select, table, count):
    total = dot(select, table)
    width = total.shape[1] // count
    return [halves(total[:, i * width : (i + 1) * width]) for i in range(count)]


def put_sent(e_ref, o_ref, slabs):
    rows = slabs[0].shape[0] // 2
    for i, s in enumerate(slabs):
        e_ref[i * rows : (i + 1) * rows, :] = s[:rows]
        o_ref[i * rows : (i + 1) * rows, :] = s[rows:]


def at_sent(sent_ref, values):
    every = jnp.concatenate([split(v) for v in values], axis=1)
    return spread(sent_ref[...], every, len(values))


def body(
    source, elem_scale, diag_block, block_inverse, face_flux, time_trace, neighbours, send_rows
):
    slabs, elements, width = source.shape
    faces = neighbours.shape[1]
    sent = send_rows.shape[1]
    halo = sent // 2
    groups = lax.axis_size("tm")
    ring = lax.axis_size("space")
    flat = source.reshape(slabs * elements, width)
    scale_row = elem_scale.reshape(1, elements)
    faces_row = neighbours.T
    stack = W_TIME + groups - 1
    full = ((elements, width), F32)
    two = ((slabs * elements, width), F32)
    edge = ((slabs * halo, width), F32)
    far = faces * sent

    swap_e = [(i, i ^ 1) for i in range(ring)]
    swap_o = [(i, (i + 1) % ring if i % 2 else (i - 1) % ring) for i in range(ring)]

    def over_e(x):
        return lax.ppermute(x, "space", swap_e)

    def over_o(x):
        return lax.ppermute(x, "space", swap_o)

    def later(x, by):
        return lax.ppermute(x, "tm", [(i, (i + by) % groups) for i in range(groups)])

    def sent_faces(picks_ref, w_ref, parts, start):
        near = None
        for f in range(faces):
            picked = dot(picks_ref[f * sent + start : (f + 1) * sent, :], parts).astype(BF16)
            term = dot(picked, w_ref[W_FACE + f])
            near = term if near is None else near + term
        return halves(near)

    def sent_at(send_ref, i):
        first = jnp.where(lax.axis_index("space") % 2 == 0, halo, 0)
        return send_ref[0, lax.rem(first + i, sent)]

    def first_kernel(
        s_hbm, scale_hbm, inv_hbm, send_hbm, e_ref, o_ref, xa_ref, xb_ref,
        s_ref, scale_ref, inv_ref, send_ref, g_ref, sems,
    ):
        copies = fetch(
            [(scale_hbm, scale_ref), (send_hbm, send_ref), (s_hbm, s_ref), (inv_hbm, inv_ref)],
            sems,
        )
        copies[0].wait()
        sigma = DAMPING / column(scale_ref[...], width)
        copies[1].wait()
        copies[2].wait()
        refs = [xa_ref, xb_ref]
        for t in range(slabs):
            refs[t][...] = s_ref[t * elements : (t + 1) * elements, :] * sigma
        for i in range(sent):
            at = sent_at(send_ref, i)
            base = (i // halo) * slabs * halo + i % halo
            for t in range(slabs):
                g_ref[base + t * halo : base + t * halo + 1, :] = refs[t][pl.ds(at, 1), :]
        copies[3].wait()
        out = dot32(g_ref[...], inv_ref[...])
        e_ref[...] = out[: slabs * halo]
        o_ref[...] = out[slabs * halo :]

    e0, o0, xa, xb = call(
        first_kernel,
        [edge, edge, full, full],
        [flat, scale_row, block_inverse, send_rows],
        spaces=[HBM] * 4,
        scratch=[
            VMEM((slabs * elements, width), F32),
            VMEM((1, elements), F32),
            VMEM((width, width), F32),
            SMEM((1, sent), jnp.int32),
            VMEM((slabs * sent, width), F32),
            pltpu.SemaphoreType.DMA((4,)),
        ],
        flops=1e7,
    )
    before = later(xb, 1)
    re0, ro0 = over_e(e0), over_o(o0)

    def setup_kernel(
        xa_ref, xb_ref, scale_hbm, d_hbm, inv_hbm, f_hbm, t_hbm, nbr_hbm, send_hbm,
        v_ref, part_ref, psent_ref, sigs_ref, fracs_ref, w_ref, pick_ref, picks_ref, q_ref, qs_ref,
        qo_ref, sent_ref, sig_ref, frac_ref,
        scale_ref, d_ref, inv_ref, f_ref, t_ref, nbr_ref, send_ref, rows_ref, sems,
    ):
        copies = fetch(
            [
                (inv_hbm, inv_ref), (t_hbm, t_ref), (d_hbm, d_ref), (f_hbm, f_ref),
                (scale_hbm, scale_ref), (nbr_hbm, nbr_ref), (send_hbm, send_ref),
            ],
            sems,
        )
        for c in copies:
            c.wait()
        inv = inv_ref[...]
        trace = dot32(t_ref[...], inv)
        w_ref[W_DIAG] = weight_tile(dot32(d_ref[...], inv))
        for f in range(faces):
            w_ref[W_FACE + f] = weight_tile(dot32(f_ref[f], inv))
        w_ref[W_SOURCE_TIME] = weight_tile(dot32(inv, trace))
        power = trace
        for a in range(groups - 1):
            w_ref[W_TIME + a] = weight_tile(power)
            if a < groups - 2:
                power = dot32(power, trace)
        scale = column(scale_ref[...], width)
        sigma = DAMPING / scale
        sig_ref[...] = sigma
        frac = 1.0 / (2.0 * scale - 1.0)
        frac_ref[...] = frac
        lane = lax.broadcasted_iota(jnp.int32, (elements, elements), 1)
        spot = lax.broadcasted_iota(jnp.int32, (elements, far), 1)
        wanted = jnp.zeros((elements, far), jnp.int32)
        for f in range(faces):
            wide = column(nbr_ref[f : f + 1, :], elements)
            pick_ref[f * elements : (f + 1) * elements, :] = jnp.where(
                wide == lane, 1.0, 0.0
            ).astype(BF16)
            wanted = jnp.where(spot // sent == f, column(nbr_ref[f : f + 1, :], far), wanted)
        q = jnp.where(wanted == elements + spot % sent, 1.0, 0.0).astype(BF16)
        q_ref[...] = q
        strip = lax.broadcasted_iota(jnp.int32, (1, elements), 1)
        for i in range(sent):
            rows_ref[i : i + 1, :] = jnp.where(strip == sent_at(send_ref, i), 1.0, 0.0)
        chosen = rows_ref[...].astype(BF16)
        sent_ref[...] = chosen
        qs = dot(chosen, q)
        qs_ref[...] = qs.astype(BF16)
        for f in range(faces):
            picks_ref[f * sent : (f + 1) * sent, :] = dot(
                chosen, pick_ref[f * elements : (f + 1) * elements, :]
            ).astype(BF16)
        head = weight_tile(inv)
        v = [product(split(x[...]), head) for x in (xa_ref, xb_ref)]
        cut = [split(x) for x in v]
        near = own_faces(faces, pick_ref, w_ref, cut)
        parts = []
        for t in range(slabs):
            term = near[t]
            if t:
                term = term + product(cut[t - 1], w_ref[W_TIME])
            parts.append(
                2.0 * v[t] - DAMPING * product(cut[t], w_ref[W_DIAG]) + sigma * term
            )
            v_ref[t * elements : (t + 1) * elements, :] = v[t]
            part_ref[t * elements : (t + 1) * elements, :] = parts[t]
        got = at_sent(sent_ref, parts + [sigma, frac])
        for t in range(slabs):
            psent_ref[t * sent : (t + 1) * sent, :] = got[t]
        sigs_ref[...] = got[slabs]
        fracs_ref[...] = got[slabs + 1]
        near_half = lax.broadcasted_iota(jnp.int32, (halo, far), 1) % sent < halo
        even = lax.axis_index("space") % 2 == 0
        kept = jnp.where(near_half, jnp.where(even, 1.0, 0.0), jnp.where(even, 0.0, 1.0))
        qo_ref[...] = got[slabs + 1][halo:] * qs[halo:] * kept

    (
        v0, part1, psent1, sig_sent, frac_sent, weights, pick, pick_sent, q_all, q_sent, q_o, choose,
        sigma_all, frac_all,
    ) = call(
        setup_kernel,
        [
            two, two, ((slabs * sent, width), F32), ((sent, width), F32), ((sent, width), F32),
            ((stack, 2 * width, 2 * width), BF16), ((faces * elements, elements), BF16),
            ((faces * sent, elements), BF16), ((elements, far), BF16), ((sent, far), BF16),
            ((halo, far), F32), ((sent, elements), BF16), full, full,
        ],
        [
            xa, xb, scale_row, diag_block, block_inverse, face_flux, time_trace, faces_row,
            send_rows,
        ],
        spaces=[VMEM] * 2 + [HBM] * 7,
        scratch=[
            VMEM((1, elements), F32),
            VMEM((width, width), F32),
            VMEM((width, width), F32),
            VMEM((faces, width, width), F32),
            VMEM((width, width), F32),
            VMEM((faces, elements), jnp.int32),
            SMEM((1, sent), jnp.int32),
            VMEM((sent, elements), F32),
            pltpu.SemaphoreType.DMA((7,)),
        ],
        flops=2e9,
    )

    def time_mask(x, by=1):
        return jnp.where(lax.axis_index("tm") >= by, x, jnp.zeros_like(x))

    def edge_one(
        re_ref, ro_ref, b_ref, psent_ref, sigs_ref, w_ref, qs_ref, sent_ref, e_ref, o_ref
    ):
        table = far_faces(faces, arrived(re_ref, ro_ref, slabs), w_ref)
        add = spread(qs_ref[...], table, slabs)
        picked = dot(sent_ref[...], split(b_ref[...])).astype(BF16)
        old = time_mask(product(picked, w_ref[W_SOURCE_TIME]))
        sig = sigs_ref[...]
        new = [psent_ref[t * sent : (t + 1) * sent, :] + sig * add[t] for t in range(slabs)]
        new[0] = new[0] + sig * old
        put_sent(e_ref, o_ref, new)

    e1, vo = call(
        edge_one,
        [edge, edge],
        [re0, ro0, before, psent1, sig_sent, weights, q_sent, choose],
        flops=1e7,
    )
    re1 = over_e(e1)

    def ahead(
        re_ref, ro_ref, b_ref, part_ref, vo_ref, o0_ref, w_ref, picks_ref, q_ref, sig_ref,
        sigs_ref, fracs_ref, v1_ref, wo_ref,
    ):
        sigma = sig_ref[...]
        add = spread(q_ref[...], far_faces(faces, arrived(re_ref, ro_ref, slabs), w_ref), slabs)
        old = time_mask(product(split(b_ref[...]), w_ref[W_SOURCE_TIME]))
        va = part_ref[:elements, :] + sigma * add[0] + sigma * old
        vb = part_ref[elements:, :] + sigma * add[1]
        v1_ref[:elements, :] = va
        v1_ref[elements:, :] = vb
        near = sent_faces(picks_ref, w_ref, split(va + vb), halo)
        sa, sb = vo_ref[:halo, :], vo_ref[halo:, :]
        rest = (
            o0_ref[:halo, :] + o0_ref[halo:, :] - DAMPING * product(split(sa + sb), w_ref[W_DIAG])
        ) / sigs_ref[halo:, :]
        rest = rest + product(split(sa), w_ref[W_TIME]) + near
        wo_ref[...] = fracs_ref[halo:, :] * rest + sb

    v1, w_part = call(
        ahead,
        [two, ((halo, width), F32)],
        [
            re0, ro0, before, part1, vo, o0, weights, pick_sent, q_all, sigma_all, sig_sent,
            frac_sent,
        ],
        flops=2e8,
    )

    def edge_w(re_ref, wo_ref, vo_ref, w_ref, qs_ref, fracs_ref, qo_ref, o_ref):
        both = re_ref[:halo, :] + re_ref[halo:, :]
        none = jnp.zeros_like(both)
        even = lax.axis_index("space") % 2 == 0
        rows = jnp.concatenate([jnp.where(even, none, both), jnp.where(even, both, none)], axis=0)
        add = spread(qs_ref[halo:, :], far_faces(faces, [rows], w_ref), 1)[0]
        frac = fracs_ref[halo:, :]
        o_ref[: slabs * halo, :] = vo_ref[...]
        o_ref[slabs * halo : (slabs + 1) * halo, :] = wo_ref[...] + frac * add
        o_ref[(slabs + 1) * halo : (slabs + 2) * halo, :] = qo_ref[...]
        o_ref[(slabs + 2) * halo :, :] = frac

    (o1,) = call(
        edge_w,
        [(((slabs + 3) * halo, width), F32)],
        [re1, w_part, vo, weights, q_sent, frac_sent, q_o],
        flops=1e7,
    )
    ro1 = over_o(o1)

    def carry(v1_ref, v_ref, w_ref, sig_ref, x_ref):
        step = split(v1_ref[:elements, :] - v1_ref[elements:, :])
        x_ref[...] = v_ref[elements:, :] + sig_ref[...] * product(step, w_ref[W_TIME])

    (x_own,) = call(carry, [full], [v1, v0, weights, sigma_all], flops=1e8)
    x_before = later(x_own, 1)

    def middle(
        v1_ref, v_ref, w_ref, pick_ref, sig_ref, frac_ref, pa_ref, pb_ref, wp_ref
    ):
        sigma = sig_ref[...]
        frac = frac_ref[...]
        va, vb = v1_ref[:elements, :], v1_ref[elements:, :]
        v0a, v0b = v_ref[:elements, :], v_ref[elements:, :]
        ca, cb = split(va), split(vb)
        ga, gb = own_faces(faces, pick_ref, w_ref, [ca, cb])
        da, db = product(ca, w_ref[W_DIAG]), product(cb, w_ref[W_DIAG])
        ta = product(ca, w_ref[W_TIME])
        pa_ref[...] = va + v0a - DAMPING * da + sigma * ga
        pb_ref[...] = vb + v0b - DAMPING * db + sigma * (ta + gb)
        wp_ref[...] = (
            frac * (((v0a + v0b) - DAMPING * (da + db)) / sigma + ta + ga + gb) + vb
        )

    pa0, pb0, wp = call(middle, [full] * 3, [v1, v0, weights, pick, sigma_all, frac_all], flops=1e9)

    more = ((elements + halo, width), F32)

    def coarse_kernel(re_ref, ro_ref, vo_ref, wp_ref, w_ref, q_ref, frac_ref, w_out, table_ref):
        rows = arrived(re_ref, ro_ref.at[: slabs * halo, :], slabs)
        both = vo_ref[:halo, :] + vo_ref[halo:, :]
        rows.append(jnp.concatenate([both, both], axis=0))
        table = far_faces(faces, rows, w_ref)
        lanes = 2 * width
        add = spread(q_ref[...], table[:, : slabs * lanes], slabs)
        mine = halves(table[:, slabs * lanes :].astype(F32))
        w_out[:elements, :] = wp_ref[...] + frac_ref[...] * (add[0] + add[1])
        w_out[elements:, :] = ro_ref[slabs * halo : (slabs + 1) * halo, :] + dot32(
            ro_ref[(slabs + 1) * halo : (slabs + 2) * halo, :], mine
        )
        table_ref[...] = table[:, : slabs * lanes]

    w_own, table1 = call(
        coarse_kernel,
        [more, ((far, slabs * 2 * width), BF16)],
        [re1, ro1, vo, wp, weights, q_all, frac_all],
        flops=1e7,
    )

    def rest_kernel(table_ref, pa_ref, pb_ref, q_ref, sig_ref, sent_ref, pa_out, pb_out, ps_out):
        add = spread(q_ref[...], table_ref[...], slabs)
        a = pa_ref[...] + sig_ref[...] * add[0]
        b = pb_ref[...] + sig_ref[...] * add[1]
        pa_out[...] = a
        pb_out[...] = b
        got = at_sent(sent_ref, [a, b])
        ps_out[:sent, :] = got[0]
        ps_out[sent:, :] = got[1]

    pa1, pb1, psent2 = call(
        rest_kernel,
        [full, full, ((slabs * sent, width), F32)],
        [table1, pa0, pb0, q_all, sigma_all, choose],
        flops=1e8,
    )
    earlier = [later(w_own, a) for a in range(1, groups)]

    def recur(*refs):
        olds = refs[: groups - 1]
        w_own_ref, v1_ref, ro_ref, w_ref, sent_ref, frac_ref, c_ref, d_ref, s_ref, e_ref, oh_ref = (
            refs[groups - 1 :]
        )
        frac = jnp.concatenate([frac_ref[...], ro_ref[(slabs + 2) * halo :, :]], axis=0)
        v_last = jnp.concatenate(
            [v1_ref[(slabs - 1) * elements :, :], ro_ref[(slabs - 1) * halo : slabs * halo, :]],
            axis=0,
        )
        d = time_mask(olds[0][...])
        c = w_own_ref[...] - v_last
        power = frac
        for a in range(1, groups):
            cut = split(time_mask(power * olds[a - 1][...], a))
            c = c + product(cut, w_ref[W_TIME + a - 1])
            if a < groups - 1:
                cut = split(time_mask(power * olds[a][...], a + 1))
                d = d + product(cut, w_ref[W_TIME + a - 1])
                power = power * frac
        c_ref[...] = c[:elements]
        d_ref[...] = d[:elements]
        oh_ref[:halo, :] = c[elements:]
        oh_ref[halo:, :] = d[elements:]
        every = jnp.concatenate([split(c[:elements]), split(d[:elements])], axis=1)
        got = spread(sent_ref[...], every, 2)
        e_ref[:halo, :] = got[0][:halo]
        e_ref[halo:, :] = got[1][:halo]
        s_ref[:sent, :] = got[0]
        s_ref[sent:, :] = got[1]

    c_all, d_all, cd_sent, e2, ro2 = call(
        recur,
        [full, full, ((2 * sent, width), F32), edge, edge],
        [*earlier, w_own, v1, ro1, weights, choose, frac_all],
        flops=1e8,
    )
    re2 = over_e(e2)

    def ahead_two(c_ref, cds_ref, ps_ref, w_ref, picks_ref, sigs_ref, out_ref):
        sigma = sigs_ref[...]
        near = sent_faces(picks_ref, w_ref, split(c_ref[...]), 0)
        c = cds_ref[:sent, :]
        cut = split(c)
        same = c - DAMPING * product(cut, w_ref[W_DIAG]) + sigma * near
        out_ref[:sent, :] = ps_ref[:sent, :] + same + sigma * product(
            split(cds_ref[sent:, :]), w_ref[W_TIME]
        )
        out_ref[sent:, :] = ps_ref[sent:, :] + same + sigma * product(cut, w_ref[W_TIME])

    (psent3,) = call(
        ahead_two,
        [((slabs * sent, width), F32)],
        [c_all, cd_sent, psent2, weights, pick_sent, sig_sent],
        flops=1e8,
    )

    def edge_two(re_ref, ro_ref, psent_ref, sigs_ref, w_ref, qs_ref, e_ref, o_ref):
        table = far_faces(faces, arrived(re_ref, ro_ref, 2)[:1], w_ref)
        add = sigs_ref[...] * spread(qs_ref[...], table, 1)[0]
        put_sent(
            e_ref, o_ref, [psent_ref[t * sent : (t + 1) * sent, :] + add for t in range(slabs)]
        )

    e3, o3 = call(
        edge_two,
        [edge, edge],
        [re2, ro2, psent3, sig_sent, weights, q_sent],
        flops=1e7,
    )
    re3, ro3 = over_e(e3), over_o(o3)

    def sweep(
        re_ref, ro_ref, c_in, d_in, xb_ref, pa_ref, pb_ref, v_ref, w_ref, pick_ref, q_ref, sig_ref,
        out_ref,
    ):
        sigma = sig_ref[...]
        c, d = c_in[...], d_in[...]
        cc, cd = split(c), split(d)
        gc, gd = own_faces(faces, pick_ref, w_ref, [cc, cd])
        add = spread(q_ref[...], far_faces(faces, arrived(re_ref, ro_ref, 2), w_ref), 2)
        same = c - DAMPING * product(cc, w_ref[W_DIAG]) + sigma * (gc + add[0])
        td = product(cd, w_ref[W_TIME])
        a = pa_ref[...] + same + sigma * td
        b = pb_ref[...] + same + sigma * product(cc, w_ref[W_TIME])
        z = (
            time_mask(xb_ref[...])
            + d
            - DAMPING * product(cd, w_ref[W_DIAG])
            + sigma * (td + gd + add[1])
        )
        ca, cb = split(a), split(b)
        ga, gb = own_faces(faces, pick_ref, w_ref, [ca, cb])
        tz, ta = product(split(z), w_ref[W_TIME]), product(ca, w_ref[W_TIME])
        out_ref[:elements, :] = (
            a + v_ref[:elements, :] - DAMPING * product(ca, w_ref[W_DIAG]) + sigma * (tz + ga)
        )
        out_ref[elements:, :] = (
            b + v_ref[elements:, :] - DAMPING * product(cb, w_ref[W_DIAG]) + sigma * (ta + gb)
        )

    (part4,) = call(
        sweep,
        [two],
        [re2, ro2, c_all, d_all, x_before, pa1, pb1, v0, weights, pick, q_all, sigma_all],
        flops=2e9,
    )

    def last(re_ref, ro_ref, p_ref, w_ref, q_ref, sig_ref, out_hbm, out_ref, sems):
        table = far_faces(faces, arrived(re_ref, ro_ref, slabs), w_ref)
        lanes = 2 * width
        copies = []
        for t in range(slabs):
            rows = pl.ds(t * elements, elements)
            add = spread(q_ref[...], table[:, t * lanes : (t + 1) * lanes], 1)[0]
            out_ref[t * elements : (t + 1) * elements, :] = (
                p_ref[t * elements : (t + 1) * elements, :] + sig_ref[...] * add
            )
            copies.append(
                pltpu.make_async_copy(out_ref.at[rows, :], out_hbm.at[rows, :], sems.at[t])
            )
            copies[-1].start()
        for c in copies:
            c.wait()

    (out,) = call(
        last,
        [two],
        [re3, ro3, part4, weights, q_all, sigma_all],
        scratch=[VMEM((slabs * elements, width), F32), pltpu.SemaphoreType.DMA((slabs,))],
        flops=1e7,
        out_space=HBM,
    )
    return out.reshape(slabs, elements, width)


def solution(mesh):
    in_specs = (
        P("tm", "space", None),
        P("space"),
        P(),
        P(),
        P(),
        P(),
        P("space", None),
        P("space", None),
    )
    out_specs = P("tm", "space", None)
    return jax.shard_map(body, mesh=mesh, in_specs=in_specs, out_specs=out_specs, check_vma=False)
```

```python
import jax
import jax.numpy as jnp
from jax import lax
from jax.experimental import pallas as pl
from jax.experimental.pallas import tpu as pltpu
from jax.sharding import PartitionSpec as P


DAMPING = 0.7
F32 = jnp.float32
BF16 = jnp.bfloat16
VMEM = pltpu.VMEM
SMEM = pltpu.SMEM
HBM = pltpu.MemorySpace.HBM

W_DIAG, W_FACE, W_SOURCE_TIME, W_TIME = 0, 1, 5, 6


def call(kernel, out_shapes, args, spaces=None, scratch=(), flops=4e8, out_space=VMEM):
    spaces = spaces or [VMEM] * len(args)
    args = [
        pltpu.with_memory_space_constraint(x, HBM) if s is HBM else x for x, s in zip(args, spaces)
    ]
    return pl.pallas_call(
        kernel,
        out_shape=[jax.ShapeDtypeStruct(s, d) for s, d in out_shapes],
        in_specs=[pl.BlockSpec(memory_space=s) for s in spaces],
        out_specs=[pl.BlockSpec(memory_space=out_space)] * len(out_shapes),
        scratch_shapes=list(scratch),
        compiler_params=pltpu.CompilerParams(vmem_limit_bytes=24 << 20),
        cost_estimate=pl.CostEstimate(flops=int(flops), bytes_accessed=1 << 20, transcendentals=0),
    )(*args)


def fetch(pairs, sems):
    copies = [pltpu.make_async_copy(a, b, sems.at[i]) for i, (a, b) in enumerate(pairs)]
    for c in copies:
        c.start()
    return copies


def split(x):
    head = x.astype(BF16)
    tail = (x - head.astype(F32)).astype(BF16)
    return jnp.concatenate([head, tail], axis=1)


def halves(x):
    width = x.shape[1] // 2
    return x[:, :width] + x[:, width:]


def dot(left, right):
    return jnp.dot(left, right, preferred_element_type=F32)


def dot32(left, right):
    return jnp.dot(left, right, precision=lax.Precision.HIGHEST, preferred_element_type=F32)


def product(parts, tile):
    return halves(dot(parts, tile))


def few(x, tile):
    head = x.astype(BF16)
    tail = (x - head.astype(F32)).astype(BF16)
    out = halves(dot(jnp.concatenate([head, tail], axis=0), tile[: x.shape[1], :]))
    return out[: x.shape[0]] + out[x.shape[0] :]


def weight_tile(w):
    head = w.astype(BF16)
    tail = (w - head.astype(F32)).astype(BF16)
    top = jnp.concatenate([head, tail], axis=1)
    low = jnp.concatenate([head, jnp.zeros_like(head)], axis=1)
    return jnp.concatenate([top, low], axis=0)


def column(row, width):
    return jnp.transpose(jnp.broadcast_to(row, (width, row.shape[1])))


def own_faces(faces, pick_ref, weights_ref, parts):
    count = len(parts)
    width = parts[0].shape[1]
    rows = parts[0].shape[0]
    every = jnp.concatenate(parts, axis=1) if count > 1 else parts[0]
    sums = [None] * count
    for face in range(faces):
        picked = dot(pick_ref[face * rows : (face + 1) * rows, :], every).astype(BF16)
        for i in range(count):
            term = dot(picked[:, i * width : (i + 1) * width], weights_ref[W_FACE + face])
            sums[i] = term if sums[i] is None else sums[i] + term
    return [halves(s) for s in sums]


def arrived(from_e, from_o, count):
    even = lax.axis_index("space") % 2 == 0
    left = jnp.where(even, from_o[...], from_e[...])
    right = jnp.where(even, from_e[...], from_o[...])
    rows = left.shape[0] // count
    return [
        jnp.concatenate([left[i * rows : (i + 1) * rows], right[i * rows : (i + 1) * rows]], axis=0)
        for i in range(count)
    ]


def far_faces(faces, rows_in, weights_ref):
    count = len(rows_in)
    n = rows_in[0].shape[0]
    rows = jnp.concatenate(rows_in, axis=0) if count > 1 else rows_in[0]
    per_face = [few(rows, weights_ref.at[W_FACE + f]) for f in range(faces)]
    lanes = [
        split(jnp.concatenate([u[i * n : (i + 1) * n] for u in per_face], axis=0))
        for i in range(count)
    ]
    return jnp.concatenate(lanes, axis=1) if count > 1 else lanes[0]


def spread(select, table, count):
    total = dot(select, table)
    width = total.shape[1] // count
    return [halves(total[:, i * width : (i + 1) * width]) for i in range(count)]


def put_sent(e_ref, o_ref, slabs):
    rows = slabs[0].shape[0] // 2
    for i, s in enumerate(slabs):
        e_ref[i * rows : (i + 1) * rows, :] = s[:rows]
        o_ref[i * rows : (i + 1) * rows, :] = s[rows:]


def at_sent(sent_ref, values):
    every = jnp.concatenate([split(v) for v in values], axis=1)
    return spread(sent_ref[...], every, len(values))


def body(
    source, elem_scale, diag_block, block_inverse, face_flux, time_trace, neighbours, send_rows
):
    slabs, elements, width = source.shape
    faces = neighbours.shape[1]
    sent = send_rows.shape[1]
    halo = sent // 2
    groups = lax.axis_size("tm")
    ring = lax.axis_size("space")
    flat = source.reshape(slabs * elements, width)
    scale_row = elem_scale.reshape(1, elements)
    faces_row = neighbours.T
    stack = W_TIME + groups - 1
    full = ((elements, width), F32)
    two = ((slabs * elements, width), F32)
    edge = ((slabs * halo, width), F32)
    far = faces * sent

    swap_e = [(i, i ^ 1) for i in range(ring)]
    swap_o = [(i, (i + 1) % ring if i % 2 else (i - 1) % ring) for i in range(ring)]

    def over_e(x):
        return lax.ppermute(x, "space", swap_e)

    def over_o(x):
        return lax.ppermute(x, "space", swap_o)

    def later(x, by):
        return lax.ppermute(x, "tm", [(i, (i + by) % groups) for i in range(groups)])

    def sent_faces(picks_ref, w_ref, parts, start):
        near = None
        for f in range(faces):
            picked = dot(picks_ref[f * sent + start : (f + 1) * sent, :], parts).astype(BF16)
            term = dot(picked, w_ref[W_FACE + f])
            near = term if near is None else near + term
        return halves(near)

    def sent_at(send_ref, i):
        first = jnp.where(lax.axis_index("space") % 2 == 0, halo, 0)
        return send_ref[0, lax.rem(first + i, sent)]

    pieces = 2
    piece = elements // pieces

    def first_kernel(
        s_hbm, scale_hbm, inv_hbm, send_hbm, d_hbm, f_hbm, t_hbm, nbr_hbm,
        e_ref, o_ref, xa_ref, xb_ref, col_ref, inv_ref, fold_ref, nbr_ref,
        s_ref, scale_ref, send_ref, g_ref, sems,
    ):
        parts = [pl.ds(i * piece, piece) for i in range(slabs * pieces)]
        pairs = [(scale_hbm, scale_ref), (send_hbm, send_ref)]
        pairs += [(s_hbm.at[p, :], s_ref.at[p, :]) for p in parts]
        pairs += [
            (inv_hbm, inv_ref),
            (d_hbm, fold_ref.at[:width, :]),
            (f_hbm, fold_ref.at[width : (faces + 1) * width, :]),
            (t_hbm, fold_ref.at[(faces + 1) * width :, :]),
            (nbr_hbm, nbr_ref),
        ]
        copies = fetch(pairs, sems)
        copies[0].wait()
        scale = column(scale_ref[...], width)
        col_ref[...] = scale
        sigma = DAMPING / scale
        for c in copies[1 : 2 + slabs * pieces]:
            c.wait()
        refs = [xa_ref, xb_ref]
        for t in range(slabs):
            refs[t][...] = s_ref[t * elements : (t + 1) * elements, :] * sigma
        for i in range(sent):
            at = sent_at(send_ref, i)
            base = (i // halo) * slabs * halo + i % halo
            for t in range(slabs):
                g_ref[base + t * halo : base + t * halo + 1, :] = refs[t][pl.ds(at, 1), :]
        copies[2 + slabs * pieces].wait()
        out = dot32(g_ref[...], inv_ref[...])
        e_ref[...] = out[: slabs * halo]
        o_ref[...] = out[slabs * halo :]
        for c in copies[3 + slabs * pieces :]:
            c.wait()

    e0, o0, xa, xb, scale_col, inv_here, fold, faces_here = call(
        first_kernel,
        [
            edge, edge, full, full, full, ((width, width), F32),
            (((faces + 2) * width, width), F32), ((faces, elements), jnp.int32),
        ],
        [
            flat, scale_row, block_inverse, send_rows, diag_block,
            face_flux.reshape(faces * width, width), time_trace, faces_row,
        ],
        spaces=[HBM] * 8,
        scratch=[
            VMEM((slabs * elements, width), F32),
            VMEM((1, elements), F32),
            SMEM((1, sent), jnp.int32),
            VMEM((slabs * sent, width), F32),
            pltpu.SemaphoreType.DMA((slabs * pieces + 7,)),
        ],
        flops=1e7,
    )
    before = later(xb, 1)
    re0, ro0 = over_e(e0), over_o(o0)

    def setup_kernel(
        xa_ref, xb_ref, col_ref, inv_ref, fold_ref, nbr_ref, send_hbm,
        v_ref, part_ref, psent_ref, sigs_ref, fracs_ref, w_ref, pick_ref, picks_ref, q_ref, qs_ref,
        qo_ref, sent_ref, back_ref, sig_ref, frac_ref,
        send_ref, line_ref, rows_ref, sems,
    ):
        copies = fetch([(send_hbm, send_ref), (send_hbm, line_ref)], sems)
        head = weight_tile(inv_ref[...])
        folded = product(split(fold_ref[...]), head)
        for i in range(faces + 1):
            w_ref[W_DIAG + i] = weight_tile(folded[i * width : (i + 1) * width])
        trace = folded[(faces + 1) * width :]
        step = weight_tile(trace)
        w_ref[W_TIME] = step
        power = trace
        for a in range(1, groups - 1):
            if a == 1:
                both = product(split(jnp.concatenate([inv_ref[...], trace], axis=0)), step)
                w_ref[W_SOURCE_TIME] = weight_tile(both[:width])
                power = both[width:]
            else:
                power = product(split(power), step)
            w_ref[W_TIME + a] = weight_tile(power)
        if groups < 3:
            w_ref[W_SOURCE_TIME] = weight_tile(product(split(inv_ref[...]), step))
        scale = col_ref[...]
        sigma = DAMPING / scale
        sig_ref[...] = sigma
        frac = 1.0 / (2.0 * scale - 1.0)
        frac_ref[...] = frac
        lane = lax.broadcasted_iota(jnp.int32, (elements, far), 1)
        spot = lax.broadcasted_iota(jnp.int32, (elements, far), 1)
        wanted = jnp.zeros((elements, far), jnp.int32)
        for f in range(faces):
            wide = column(nbr_ref[f : f + 1, :], far)
            for base in range(0, elements, far):
                pick_ref[f * elements : (f + 1) * elements, base : base + far] = jnp.where(
                    wide == lane + base, 1.0, 0.0
                ).astype(BF16)
            wanted = jnp.where(spot // sent == f, wide, wanted)
        q = jnp.where(wanted == elements + spot % sent, 1.0, 0.0).astype(BF16)
        q_ref[...] = q
        strip = lax.broadcasted_iota(jnp.int32, (1, elements), 1)
        for c in copies:
            c.wait()
        row = lax.broadcasted_iota(jnp.int32, (elements, sent), 0)
        back_ref[...] = jnp.where(row == line_ref[...], 1.0, 0.0).astype(BF16)
        for i in range(sent):
            rows_ref[i : i + 1, :] = jnp.where(strip == sent_at(send_ref, i), 1.0, 0.0)
        chosen = rows_ref[...].astype(BF16)
        sent_ref[...] = chosen
        qs = dot(chosen, q)
        qs_ref[...] = qs.astype(BF16)
        for f in range(faces):
            picks_ref[f * sent : (f + 1) * sent, :] = dot(
                chosen, pick_ref[f * elements : (f + 1) * elements, :]
            ).astype(BF16)
        v = [product(split(x[...]), head) for x in (xa_ref, xb_ref)]
        cut = [split(x) for x in v]
        near = own_faces(faces, pick_ref, w_ref, cut)
        parts = []
        for t in range(slabs):
            term = near[t]
            if t:
                term = term + product(cut[t - 1], w_ref[W_TIME])
            parts.append(
                2.0 * v[t] - DAMPING * product(cut[t], w_ref[W_DIAG]) + sigma * term
            )
            v_ref[t * elements : (t + 1) * elements, :] = v[t]
            part_ref[t * elements : (t + 1) * elements, :] = parts[t]
        got = at_sent(sent_ref, parts + [sigma, frac])
        for t in range(slabs):
            psent_ref[t * sent : (t + 1) * sent, :] = got[t]
        sigs_ref[...] = got[slabs]
        fracs_ref[...] = got[slabs + 1]
        near_half = lax.broadcasted_iota(jnp.int32, (halo, far), 1) % sent < halo
        even = lax.axis_index("space") % 2 == 0
        kept = jnp.where(near_half, jnp.where(even, 1.0, 0.0), jnp.where(even, 0.0, 1.0))
        qo_ref[...] = qs[halo:] * kept

    (
        v0, part1, psent1, sig_sent, frac_sent, weights, pick, pick_sent, q_all, q_sent, q_o, choose,
        put_back, sigma_all, frac_all,
    ) = call(
        setup_kernel,
        [
            two, two, ((slabs * sent, width), F32), ((sent, width), F32), ((sent, width), F32),
            ((stack, 2 * width, 2 * width), BF16), ((faces * elements, elements), BF16),
            ((faces * sent, elements), BF16), ((elements, far), BF16), ((sent, far), BF16),
            ((halo, far), F32), ((sent, elements), BF16), ((elements, sent), BF16), full, full,
        ],
        [
            xa, xb, scale_col, inv_here, fold, faces_here, send_rows,
        ],
        spaces=[VMEM] * 6 + [HBM],
        scratch=[
            SMEM((1, sent), jnp.int32),
            VMEM((1, sent), jnp.int32),
            VMEM((sent, elements), F32),
            pltpu.SemaphoreType.DMA((2,)),
        ],
        flops=2e9,
    )

    def time_mask(x, by=1):
        return jnp.where(lax.axis_index("tm") >= by, x, jnp.zeros_like(x))

    def edge_one(
        re_ref, ro_ref, b_ref, psent_ref, sigs_ref, w_ref, qs_ref, sent_ref, e_ref, o_ref
    ):
        table = far_faces(faces, arrived(re_ref, ro_ref, slabs), w_ref)
        add = spread(qs_ref[...], table, slabs)
        picked = dot(sent_ref[...], split(b_ref[...])).astype(BF16)
        old = time_mask(product(picked, w_ref[W_SOURCE_TIME]))
        sig = sigs_ref[...]
        new = [psent_ref[t * sent : (t + 1) * sent, :] + sig * add[t] for t in range(slabs)]
        new[0] = new[0] + sig * old
        put_sent(e_ref, o_ref, new)

    e1, vo = call(
        edge_one,
        [edge, edge],
        [re0, ro0, before, psent1, sig_sent, weights, q_sent, choose],
        flops=1e7,
    )
    re1 = over_e(e1)

    def ahead(
        re_ref, ro_ref, b_ref, part_ref, vo_ref, o0_ref, w_ref, picks_ref, q_ref, sig_ref,
        sigs_ref, fracs_ref, v1_ref, wo_ref,
    ):
        sigma = sig_ref[...]
        add = spread(q_ref[...], far_faces(faces, arrived(re_ref, ro_ref, slabs), w_ref), slabs)
        old = time_mask(product(split(b_ref[...]), w_ref[W_SOURCE_TIME]))
        va = part_ref[:elements, :] + sigma * add[0] + sigma * old
        vb = part_ref[elements:, :] + sigma * add[1]
        v1_ref[:elements, :] = va
        v1_ref[elements:, :] = vb
        near = sent_faces(picks_ref, w_ref, split(va + vb), halo)
        sa, sb = vo_ref[:halo, :], vo_ref[halo:, :]
        rest = (
            o0_ref[:halo, :] + o0_ref[halo:, :] - DAMPING * few(sa + sb, w_ref.at[W_DIAG])
        ) / sigs_ref[halo:, :]
        rest = rest + few(sa, w_ref.at[W_TIME]) + near
        wo_ref[...] = fracs_ref[halo:, :] * rest + sb

    v1, w_part = call(
        ahead,
        [two, ((halo, width), F32)],
        [
            re0, ro0, before, part1, vo, o0, weights, pick_sent, q_all, sigma_all, sig_sent,
            frac_sent,
        ],
        flops=2e8,
    )

    def edge_w(re_ref, wo_ref, vo_ref, w_ref, qs_ref, fracs_ref, qo_ref, o_ref):
        both = re_ref[:halo, :] + re_ref[halo:, :]
        none = jnp.zeros_like(both)
        even = lax.axis_index("space") % 2 == 0
        rows = jnp.concatenate([jnp.where(even, none, both), jnp.where(even, both, none)], axis=0)
        add = spread(qs_ref[halo:, :], far_faces(faces, [rows], w_ref), 1)[0]
        frac = fracs_ref[halo:, :]
        o_ref[: slabs * halo, :] = vo_ref[...]
        o_ref[slabs * halo : (slabs + 1) * halo, :] = wo_ref[...] + frac * add
        o_ref[(slabs + 1) * halo : (slabs + 2) * halo, :] = qo_ref[...]
        o_ref[(slabs + 2) * halo :, :] = frac

    (o1,) = call(
        edge_w,
        [(((slabs + 3) * halo, width), F32)],
        [re1, w_part, vo, weights, q_sent, frac_sent, q_o],
        flops=1e7,
    )
    ro1 = over_o(o1)

    def middle(
        v1_ref, v_ref, w_ref, pick_ref, sig_ref, frac_ref, pa_ref, pb_ref, wp_ref
    ):
        sigma = sig_ref[...]
        frac = frac_ref[...]
        va, vb = v1_ref[:elements, :], v1_ref[elements:, :]
        v0a, v0b = v_ref[:elements, :], v_ref[elements:, :]
        ca, cb = split(va), split(vb)
        ga, gb = own_faces(faces, pick_ref, w_ref, [ca, cb])
        da, db = product(ca, w_ref[W_DIAG]), product(cb, w_ref[W_DIAG])
        ta = product(ca, w_ref[W_TIME])
        pa_ref[...] = va + v0a - DAMPING * da + sigma * ga
        pb_ref[...] = vb + v0b - DAMPING * db + sigma * (ta + gb)
        wp_ref[...] = (
            frac * (((v0a + v0b) - DAMPING * (da + db)) / sigma + ta + ga + gb) + vb
        )

    pa0, pb0, wp = call(middle, [full] * 3, [v1, v0, weights, pick, sigma_all, frac_all], flops=1e9)

    early_w = [later(wp, a) for a in range(1, groups)]

    def carry(v1_ref, v_ref, w_ref, sig_ref, x_ref):
        step = split(v1_ref[:elements, :] - v1_ref[elements:, :])
        x_ref[...] = v_ref[elements:, :] + sig_ref[...] * product(step, w_ref[W_TIME])

    (x_own,) = call(carry, [full], [v1, v0, weights, sigma_all], flops=1e8)

    few_rows = ((sent + halo, width), F32)

    def coarse_kernel(re_ref, ro_ref, vo_ref, w_ref, qs_ref, fracs_ref, w_out, table_ref):
        rows = arrived(re_ref, ro_ref.at[: slabs * halo, :], slabs)
        both = vo_ref[:halo, :] + vo_ref[halo:, :]
        rows.append(jnp.concatenate([both, both], axis=0))
        table = far_faces(faces, rows, w_ref)
        lanes = 2 * width
        add = spread(qs_ref[...], table[:, : slabs * lanes], slabs)
        late = fracs_ref[...] * (add[0] + add[1])
        even = lax.axis_index("space") % 2 == 0
        w_out[:halo, :] = jnp.where(even, late[halo:], late[:halo])
        w_out[halo:sent, :] = jnp.where(even, late[:halo], late[halo:])
        mine = spread(
            ro_ref[(slabs + 1) * halo : (slabs + 2) * halo, :].astype(BF16),
            table[:, slabs * lanes :],
            1,
        )[0]
        w_out[sent:, :] = (
            ro_ref[slabs * halo : (slabs + 1) * halo, :] + ro_ref[(slabs + 2) * halo :, :] * mine
        )
        table_ref[...] = table[:, : slabs * lanes]

    w_late, table1 = call(
        coarse_kernel,
        [few_rows, ((far, slabs * 2 * width), BF16)],
        [re1, ro1, vo, weights, q_sent, frac_sent],
        flops=1e7,
    )
    late_w = [later(w_late, a) for a in range(1, groups)]
    x_before = later(x_own, 1)

    def rest_kernel(
        table_ref, pa_ref, pb_ref, wp_ref, v1_ref, q_ref, sig_ref, frac_ref, sent_ref,
        pa_out, pb_out, ps_out, c_out,
    ):
        add = spread(q_ref[...], table_ref[...], slabs)
        a = pa_ref[...] + sig_ref[...] * add[0]
        b = pb_ref[...] + sig_ref[...] * add[1]
        pa_out[...] = a
        pb_out[...] = b
        c_out[...] = (
            wp_ref[...] - v1_ref[(slabs - 1) * elements :, :] + frac_ref[...] * (add[0] + add[1])
        )
        got = at_sent(sent_ref, [a, b])
        ps_out[:sent, :] = got[0]
        ps_out[sent:, :] = got[1]

    pa1, pb1, psent2, c_start = call(
        rest_kernel,
        [full, full, ((slabs * sent, width), F32), full],
        [table1, pa0, pb0, wp, v1, q_all, sigma_all, frac_all, choose],
        flops=1e8,
    )

    def recur(*refs):
        n = groups - 1
        earlies, lates = refs[:n], refs[n : 2 * n]
        c0_ref, late_ref, ro_ref, w_ref, sent_ref, back_ref, frac_ref = refs[2 * n : 2 * n + 7]
        c_ref, d_ref, s_ref, e_ref, oh_ref = refs[2 * n + 7 :]
        every = jnp.concatenate([split(x[:sent, :]) for x in lates], axis=1)
        fixes = spread(back_ref[...], every, n)
        olds = [
            jnp.concatenate([x[...] + fix, y[sent:, :]], axis=0)
            for x, y, fix in zip(earlies, lates, fixes)
        ]
        frac = jnp.concatenate([frac_ref[...], ro_ref[(slabs + 2) * halo :, :]], axis=0)
        c = jnp.concatenate(
            [c0_ref[...], late_ref[sent:, :] - ro_ref[(slabs - 1) * halo : slabs * halo, :]], axis=0
        )
        d = time_mask(olds[0])
        power = frac
        for a in range(1, groups):
            cut = split(time_mask(power * olds[a - 1], a))
            c = c + product(cut, w_ref[W_TIME + a - 1])
            if a < groups - 1:
                cut = split(time_mask(power * olds[a], a + 1))
                d = d + product(cut, w_ref[W_TIME + a - 1])
                power = power * frac
        c_ref[...] = c[:elements]
        d_ref[...] = d[:elements]
        oh_ref[:halo, :] = c[elements:]
        oh_ref[halo:, :] = d[elements:]
        every = jnp.concatenate([split(c[:elements]), split(d[:elements])], axis=1)
        got = spread(sent_ref[...], every, 2)
        e_ref[:halo, :] = got[0][:halo]
        e_ref[halo:, :] = got[1][:halo]
        s_ref[:sent, :] = got[0]
        s_ref[sent:, :] = got[1]

    c_all, d_all, cd_sent, e2, ro2 = call(
        recur,
        [full, full, ((2 * sent, width), F32), edge, edge],
        [*early_w, *late_w, c_start, w_late, ro1, weights, choose, put_back, frac_all],
        flops=1e8,
    )
    re2 = over_e(e2)

    def ahead_two(c_ref, cds_ref, ps_ref, w_ref, picks_ref, sigs_ref, out_ref):
        sigma = sigs_ref[...]
        near = sent_faces(picks_ref, w_ref, split(c_ref[...]), 0)
        c = cds_ref[:sent, :]
        same = c - DAMPING * few(c, w_ref.at[W_DIAG]) + sigma * near
        times = few(cds_ref[...], w_ref.at[W_TIME])
        out_ref[:sent, :] = ps_ref[:sent, :] + same + sigma * times[sent:]
        out_ref[sent:, :] = ps_ref[sent:, :] + same + sigma * times[:sent]

    (psent3,) = call(
        ahead_two,
        [((slabs * sent, width), F32)],
        [c_all, cd_sent, psent2, weights, pick_sent, sig_sent],
        flops=1e8,
    )

    def near_c(c_ref, w_ref, pick_ref, g_ref):
        g_ref[...] = own_faces(faces, pick_ref, w_ref, [split(c_ref[...])])[0]

    (g_c,) = call(near_c, [full], [c_all, weights, pick], flops=3e8)

    def edge_two(re_ref, ro_ref, psent_ref, sigs_ref, w_ref, qs_ref, e_ref, o_ref):
        table = far_faces(faces, arrived(re_ref, ro_ref, 2)[:1], w_ref)
        add = sigs_ref[...] * spread(qs_ref[...], table, 1)[0]
        put_sent(
            e_ref, o_ref, [psent_ref[t * sent : (t + 1) * sent, :] + add for t in range(slabs)]
        )

    e3, o3 = call(
        edge_two,
        [edge, edge],
        [re2, ro2, psent3, sig_sent, weights, q_sent],
        flops=1e7,
    )
    re3, ro3 = over_e(e3), over_o(o3)

    def sweep(
        re_ref, ro_ref, c_in, d_in, g_ref, xb_ref, pa_ref, pb_ref, v_ref, w_ref, pick_ref, q_ref, sig_ref,
        out_ref,
    ):
        sigma = sig_ref[...]
        c, d = c_in[...], d_in[...]
        cc, cd = split(c), split(d)
        gc, gd = g_ref[...], own_faces(faces, pick_ref, w_ref, [cd])[0]
        add = spread(q_ref[...], far_faces(faces, arrived(re_ref, ro_ref, 2), w_ref), 2)
        same = c - DAMPING * product(cc, w_ref[W_DIAG]) + sigma * (gc + add[0])
        td = product(cd, w_ref[W_TIME])
        a = pa_ref[...] + same + sigma * td
        b = pb_ref[...] + same + sigma * product(cc, w_ref[W_TIME])
        z = (
            time_mask(xb_ref[...])
            + d
            - DAMPING * product(cd, w_ref[W_DIAG])
            + sigma * (td + gd + add[1])
        )
        ca, cb = split(a), split(b)
        ga, gb = own_faces(faces, pick_ref, w_ref, [ca, cb])
        tz, ta = product(split(z), w_ref[W_TIME]), product(ca, w_ref[W_TIME])
        out_ref[:elements, :] = (
            a + v_ref[:elements, :] - DAMPING * product(ca, w_ref[W_DIAG]) + sigma * (tz + ga)
        )
        out_ref[elements:, :] = (
            b + v_ref[elements:, :] - DAMPING * product(cb, w_ref[W_DIAG]) + sigma * (ta + gb)
        )

    (part4,) = call(
        sweep,
        [two],
        [re2, ro2, c_all, d_all, g_c, x_before, pa1, pb1, v0, weights, pick, q_all, sigma_all],
        flops=2e9,
    )

    def last(re_ref, ro_ref, p_ref, w_ref, q_ref, sig_ref, out_hbm, out_ref, sems):
        table = far_faces(faces, arrived(re_ref, ro_ref, slabs), w_ref)
        lanes = 2 * width
        copies = []
        for t in range(slabs):
            rows = pl.ds(t * elements, elements)
            add = spread(q_ref[...], table[:, t * lanes : (t + 1) * lanes], 1)[0]
            out_ref[t * elements : (t + 1) * elements, :] = (
                p_ref[t * elements : (t + 1) * elements, :] + sig_ref[...] * add
            )
            copies.append(
                pltpu.make_async_copy(out_ref.at[rows, :], out_hbm.at[rows, :], sems.at[t])
            )
            copies[-1].start()
        for c in copies:
            c.wait()

    (out,) = call(
        last,
        [two],
        [re3, ro3, part4, weights, q_all, sigma_all],
        scratch=[VMEM((slabs * elements, width), F32), pltpu.SemaphoreType.DMA((slabs,))],
        flops=1e7,
        out_space=HBM,
    )
    return out.reshape(slabs, elements, width)


def solution(mesh):
    in_specs = (
        P("tm", "space", None),
        P("space"),
        P(),
        P(),
        P(),
        P(),
        P("space", None),
        P("space", None),
    )
    out_specs = P("tm", "space", None)
    return jax.shard_map(body, mesh=mesh, in_specs=in_specs, out_specs=out_specs, check_vma=False)
```

```python
import jax
import jax.numpy as jnp
from jax import lax
from jax.experimental import pallas as pl
from jax.experimental.pallas import tpu as pltpu
from jax.sharding import PartitionSpec as P


DAMPING = 0.7
F32 = jnp.float32
BF16 = jnp.bfloat16
VMEM = pltpu.VMEM
SMEM = pltpu.SMEM
HBM = pltpu.MemorySpace.HBM

W_DIAG, W_FACE, W_SOURCE_TIME, W_TIME = 0, 1, 5, 6


def call(kernel, out_shapes, args, spaces=None, scratch=(), flops=4e8, out_space=VMEM):
    spaces = spaces or [VMEM] * len(args)
    args = [
        pltpu.with_memory_space_constraint(x, HBM) if s is HBM else x for x, s in zip(args, spaces)
    ]
    return pl.pallas_call(
        kernel,
        out_shape=[jax.ShapeDtypeStruct(s, d) for s, d in out_shapes],
        in_specs=[pl.BlockSpec(memory_space=s) for s in spaces],
        out_specs=[pl.BlockSpec(memory_space=out_space)] * len(out_shapes),
        scratch_shapes=list(scratch),
        compiler_params=pltpu.CompilerParams(vmem_limit_bytes=24 << 20),
        cost_estimate=pl.CostEstimate(flops=int(flops), bytes_accessed=1 << 20, transcendentals=0),
    )(*args)


def fetch(pairs, sems):
    copies = [pltpu.make_async_copy(a, b, sems.at[i]) for i, (a, b) in enumerate(pairs)]
    for c in copies:
        c.start()
    return copies


def split(x):
    head = x.astype(BF16)
    tail = (x - head.astype(F32)).astype(BF16)
    return jnp.concatenate([head, tail], axis=1)


def halves(x):
    width = x.shape[1] // 2
    return x[:, :width] + x[:, width:]


def dot(left, right):
    return jnp.dot(left, right, preferred_element_type=F32)


def dot32(left, right):
    return jnp.dot(left, right, precision=lax.Precision.HIGHEST, preferred_element_type=F32)


def product(parts, tile):
    return halves(dot(parts, tile))


def few(x, tile):
    head = x.astype(BF16)
    tail = (x - head.astype(F32)).astype(BF16)
    out = halves(dot(jnp.concatenate([head, tail], axis=0), tile[: x.shape[1], :]))
    return out[: x.shape[0]] + out[x.shape[0] :]


def weight_tile(w):
    head = w.astype(BF16)
    tail = (w - head.astype(F32)).astype(BF16)
    top = jnp.concatenate([head, tail], axis=1)
    low = jnp.concatenate([head, jnp.zeros_like(head)], axis=1)
    return jnp.concatenate([top, low], axis=0)


def column(row, width):
    return jnp.transpose(jnp.broadcast_to(row, (width, row.shape[1])))


def own_faces(faces, pick_ref, weights_ref, parts):
    count = len(parts)
    width = parts[0].shape[1]
    rows = parts[0].shape[0]
    every = jnp.concatenate(parts, axis=1) if count > 1 else parts[0]
    sums = [None] * count
    for face in range(faces):
        picked = dot(pick_ref[face * rows : (face + 1) * rows, :], every).astype(BF16)
        for i in range(count):
            term = dot(picked[:, i * width : (i + 1) * width], weights_ref[W_FACE + face])
            sums[i] = term if sums[i] is None else sums[i] + term
    return [halves(s) for s in sums]


def arrived(from_e, from_o, count):
    even = lax.axis_index("space") % 2 == 0
    left = jnp.where(even, from_o[...], from_e[...])
    right = jnp.where(even, from_e[...], from_o[...])
    rows = left.shape[0] // count
    return [
        jnp.concatenate([left[i * rows : (i + 1) * rows], right[i * rows : (i + 1) * rows]], axis=0)
        for i in range(count)
    ]


def far_faces(faces, rows_in, weights_ref):
    count = len(rows_in)
    n = rows_in[0].shape[0]
    rows = jnp.concatenate(rows_in, axis=0) if count > 1 else rows_in[0]
    per_face = [few(rows, weights_ref.at[W_FACE + f]) for f in range(faces)]
    lanes = [
        split(jnp.concatenate([u[i * n : (i + 1) * n] for u in per_face], axis=0))
        for i in range(count)
    ]
    return jnp.concatenate(lanes, axis=1) if count > 1 else lanes[0]


def spread(select, table, count):
    total = dot(select, table)
    width = total.shape[1] // count
    return [halves(total[:, i * width : (i + 1) * width]) for i in range(count)]


def put_sent(e_ref, o_ref, slabs):
    rows = slabs[0].shape[0] // 2
    for i, s in enumerate(slabs):
        e_ref[i * rows : (i + 1) * rows, :] = s[:rows]
        o_ref[i * rows : (i + 1) * rows, :] = s[rows:]


def at_sent(sent_ref, values):
    every = jnp.concatenate([split(v) for v in values], axis=1)
    return spread(sent_ref[...], every, len(values))


def body(
    source, elem_scale, diag_block, block_inverse, face_flux, time_trace, neighbours, send_rows
):
    slabs, elements, width = source.shape
    faces = neighbours.shape[1]
    sent = send_rows.shape[1]
    halo = sent // 2
    groups = lax.axis_size("tm")
    ring = lax.axis_size("space")
    flat = source.reshape(slabs * elements, width)
    scale_row = elem_scale.reshape(1, elements)
    faces_row = neighbours.T
    stack = W_TIME + groups - 1
    full = ((elements, width), F32)
    two = ((slabs * elements, width), F32)
    edge = ((slabs * halo, width), F32)
    far = faces * sent

    swap_e = [(i, i ^ 1) for i in range(ring)]
    swap_o = [(i, (i + 1) % ring if i % 2 else (i - 1) % ring) for i in range(ring)]

    def over_e(x):
        return lax.ppermute(x, "space", swap_e)

    def over_o(x):
        return lax.ppermute(x, "space", swap_o)

    def later(x, by):
        return lax.ppermute(x, "tm", [(i, (i + by) % groups) for i in range(groups)])

    def sent_faces(picks_ref, w_ref, parts, start):
        near = None
        for f in range(faces):
            picked = dot(picks_ref[f * sent + start : (f + 1) * sent, :], parts).astype(BF16)
            term = dot(picked, w_ref[W_FACE + f])
            near = term if near is None else near + term
        return halves(near)

    def sent_at(send_ref, i):
        first = jnp.where(lax.axis_index("space") % 2 == 0, halo, 0)
        return send_ref[0, lax.rem(first + i, sent)]

    pieces = 2
    piece = elements // pieces

    def first_kernel(
        s_hbm, scale_hbm, inv_hbm, send_hbm, d_hbm, f_hbm, t_hbm, nbr_hbm,
        e_ref, o_ref, xa_ref, xb_ref, col_ref, inv_ref, fold_ref, nbr_ref,
        s_ref, scale_ref, send_ref, g_ref, sems,
    ):
        parts = [pl.ds(i * piece, piece) for i in range(slabs * pieces)]
        pairs = [(scale_hbm, scale_ref), (send_hbm, send_ref)]
        pairs += [(s_hbm.at[p, :], s_ref.at[p, :]) for p in parts]
        pairs += [
            (inv_hbm, inv_ref),
            (d_hbm, fold_ref.at[:width, :]),
            (f_hbm, fold_ref.at[width : (faces + 1) * width, :]),
            (t_hbm, fold_ref.at[(faces + 1) * width :, :]),
            (nbr_hbm, nbr_ref),
        ]
        copies = fetch(pairs, sems)
        copies[0].wait()
        scale = column(scale_ref[...], width)
        col_ref[...] = scale
        sigma = DAMPING / scale
        for c in copies[1 : 2 + slabs * pieces]:
            c.wait()
        refs = [xa_ref, xb_ref]
        for t in range(slabs):
            refs[t][...] = s_ref[t * elements : (t + 1) * elements, :] * sigma
        for i in range(sent):
            at = sent_at(send_ref, i)
            base = (i // halo) * slabs * halo + i % halo
            for t in range(slabs):
                g_ref[base + t * halo : base + t * halo + 1, :] = refs[t][pl.ds(at, 1), :]
        copies[2 + slabs * pieces].wait()
        out = dot32(g_ref[...], inv_ref[...])
        e_ref[...] = out[: slabs * halo]
        o_ref[...] = out[slabs * halo :]
        for c in copies[3 + slabs * pieces :]:
            c.wait()

    e0, o0, xa, xb, scale_col, inv_here, fold, faces_here = call(
        first_kernel,
        [
            edge, edge, full, full, full, ((width, width), F32),
            (((faces + 2) * width, width), F32), ((faces, elements), jnp.int32),
        ],
        [
            flat, scale_row, block_inverse, send_rows, diag_block,
            face_flux.reshape(faces * width, width), time_trace, faces_row,
        ],
        spaces=[HBM] * 8,
        scratch=[
            VMEM((slabs * elements, width), F32),
            VMEM((1, elements), F32),
            SMEM((1, sent), jnp.int32),
            VMEM((slabs * sent, width), F32),
            pltpu.SemaphoreType.DMA((slabs * pieces + 7,)),
        ],
        flops=1e7,
    )
    before = later(xb, 1)
    re0, ro0 = over_e(e0), over_o(o0)

    def setup_kernel(
        xa_ref, xb_ref, col_ref, inv_ref, fold_ref, nbr_ref, send_hbm,
        v_ref, part_ref, psent_ref, sigs_ref, fracs_ref, w_ref, pick_ref, picks_ref, q_ref, qs_ref,
        qo_ref, sent_ref, back_ref, sig_ref, frac_ref,
        send_ref, line_ref, rows_ref, sems,
    ):
        copies = fetch([(send_hbm, send_ref), (send_hbm, line_ref)], sems)
        head = weight_tile(inv_ref[...])
        folded = product(split(fold_ref[...]), head)
        for i in range(faces + 1):
            w_ref[W_DIAG + i] = weight_tile(folded[i * width : (i + 1) * width])
        trace = folded[(faces + 1) * width :]
        step = weight_tile(trace)
        w_ref[W_TIME] = step
        power = trace
        for a in range(1, groups - 1):
            if a == 1:
                both = product(split(jnp.concatenate([inv_ref[...], trace], axis=0)), step)
                w_ref[W_SOURCE_TIME] = weight_tile(both[:width])
                power = both[width:]
            else:
                power = product(split(power), step)
            w_ref[W_TIME + a] = weight_tile(power)
        if groups < 3:
            w_ref[W_SOURCE_TIME] = weight_tile(product(split(inv_ref[...]), step))
        scale = col_ref[...]
        sigma = DAMPING / scale
        sig_ref[...] = sigma
        frac = 1.0 / (2.0 * scale - 1.0)
        frac_ref[...] = frac
        lane = lax.broadcasted_iota(jnp.int32, (elements, far), 1)
        spot = lax.broadcasted_iota(jnp.int32, (elements, far), 1)
        wanted = jnp.zeros((elements, far), jnp.int32)
        for f in range(faces):
            wide = column(nbr_ref[f : f + 1, :], far)
            for base in range(0, elements, far):
                pick_ref[f * elements : (f + 1) * elements, base : base + far] = jnp.where(
                    wide == lane + base, 1.0, 0.0
                ).astype(BF16)
            wanted = jnp.where(spot // sent == f, wide, wanted)
        q = jnp.where(wanted == elements + spot % sent, 1.0, 0.0).astype(BF16)
        q_ref[...] = q
        strip = lax.broadcasted_iota(jnp.int32, (1, elements), 1)
        for c in copies:
            c.wait()
        row = lax.broadcasted_iota(jnp.int32, (elements, sent), 0)
        back_ref[...] = jnp.where(row == line_ref[...], 1.0, 0.0).astype(BF16)
        for i in range(sent):
            rows_ref[i : i + 1, :] = jnp.where(strip == sent_at(send_ref, i), 1.0, 0.0)
        chosen = rows_ref[...].astype(BF16)
        sent_ref[...] = chosen
        qs = dot(chosen, q)
        qs_ref[...] = qs.astype(BF16)
        for f in range(faces):
            picks_ref[f * sent : (f + 1) * sent, :] = dot(
                chosen, pick_ref[f * elements : (f + 1) * elements, :]
            ).astype(BF16)
        v = [product(split(x[...]), head) for x in (xa_ref, xb_ref)]
        cut = [split(x) for x in v]
        near = own_faces(faces, pick_ref, w_ref, cut)
        parts = []
        for t in range(slabs):
            term = near[t]
            if t:
                term = term + product(cut[t - 1], w_ref[W_TIME])
            parts.append(
                2.0 * v[t] - DAMPING * product(cut[t], w_ref[W_DIAG]) + sigma * term
            )
            v_ref[t * elements : (t + 1) * elements, :] = v[t]
            part_ref[t * elements : (t + 1) * elements, :] = parts[t]
        got = at_sent(sent_ref, parts + [sigma, frac])
        for t in range(slabs):
            psent_ref[t * sent : (t + 1) * sent, :] = got[t]
        sigs_ref[...] = got[slabs]
        fracs_ref[...] = got[slabs + 1]
        near_half = lax.broadcasted_iota(jnp.int32, (halo, far), 1) % sent < halo
        even = lax.axis_index("space") % 2 == 0
        kept = jnp.where(near_half, jnp.where(even, 1.0, 0.0), jnp.where(even, 0.0, 1.0))
        qo_ref[...] = qs[halo:] * kept

    (
        v0, part1, psent1, sig_sent, frac_sent, weights, pick, pick_sent, q_all, q_sent, q_o, choose,
        put_back, sigma_all, frac_all,
    ) = call(
        setup_kernel,
        [
            two, two, ((slabs * sent, width), F32), ((sent, width), F32), ((sent, width), F32),
            ((stack, 2 * width, 2 * width), BF16), ((faces * elements, elements), BF16),
            ((faces * sent, elements), BF16), ((elements, far), BF16), ((sent, far), BF16),
            ((halo, far), F32), ((sent, elements), BF16), ((elements, sent), BF16), full, full,
        ],
        [
            xa, xb, scale_col, inv_here, fold, faces_here, send_rows,
        ],
        spaces=[VMEM] * 6 + [HBM],
        scratch=[
            SMEM((1, sent), jnp.int32),
            VMEM((1, sent), jnp.int32),
            VMEM((sent, elements), F32),
            pltpu.SemaphoreType.DMA((2,)),
        ],
        flops=2e9,
    )

    def time_mask(x, by=1):
        return jnp.where(lax.axis_index("tm") >= by, x, jnp.zeros_like(x))

    def edge_one(
        re_ref, ro_ref, b_ref, psent_ref, sigs_ref, w_ref, qs_ref, sent_ref, e_ref, o_ref
    ):
        table = far_faces(faces, arrived(re_ref, ro_ref, slabs), w_ref)
        add = spread(qs_ref[...], table, slabs)
        picked = dot(sent_ref[...], split(b_ref[...])).astype(BF16)
        old = time_mask(product(picked, w_ref[W_SOURCE_TIME]))
        sig = sigs_ref[...]
        new = [psent_ref[t * sent : (t + 1) * sent, :] + sig * add[t] for t in range(slabs)]
        new[0] = new[0] + sig * old
        put_sent(e_ref, o_ref, new)

    e1, vo = call(
        edge_one,
        [edge, edge],
        [re0, ro0, before, psent1, sig_sent, weights, q_sent, choose],
        flops=1e7,
    )
    re1 = over_e(e1)

    def ahead(
        re_ref, ro_ref, b_ref, part_ref, vo_ref, o0_ref, w_ref, picks_ref, q_ref, sig_ref,
        sigs_ref, fracs_ref, v1_ref, wo_ref,
    ):
        sigma = sig_ref[...]
        add = spread(q_ref[...], far_faces(faces, arrived(re_ref, ro_ref, slabs), w_ref), slabs)
        old = time_mask(product(split(b_ref[...]), w_ref[W_SOURCE_TIME]))
        va = part_ref[:elements, :] + sigma * add[0] + sigma * old
        vb = part_ref[elements:, :] + sigma * add[1]
        v1_ref[:elements, :] = va
        v1_ref[elements:, :] = vb
        near = sent_faces(picks_ref, w_ref, split(va + vb), halo)
        sa, sb = vo_ref[:halo, :], vo_ref[halo:, :]
        rest = (
            o0_ref[:halo, :] + o0_ref[halo:, :] - DAMPING * few(sa + sb, w_ref.at[W_DIAG])
        ) / sigs_ref[halo:, :]
        rest = rest + few(sa, w_ref.at[W_TIME]) + near
        wo_ref[...] = fracs_ref[halo:, :] * rest + sb

    v1, w_part = call(
        ahead,
        [two, ((halo, width), F32)],
        [
            re0, ro0, before, part1, vo, o0, weights, pick_sent, q_all, sigma_all, sig_sent,
            frac_sent,
        ],
        flops=2e8,
    )

    def edge_w(re_ref, wo_ref, vo_ref, w_ref, qs_ref, fracs_ref, qo_ref, o_ref):
        both = re_ref[:halo, :] + re_ref[halo:, :]
        none = jnp.zeros_like(both)
        even = lax.axis_index("space") % 2 == 0
        rows = jnp.concatenate([jnp.where(even, none, both), jnp.where(even, both, none)], axis=0)
        add = spread(qs_ref[halo:, :], far_faces(faces, [rows], w_ref), 1)[0]
        frac = fracs_ref[halo:, :]
        o_ref[: slabs * halo, :] = vo_ref[...]
        o_ref[slabs * halo : (slabs + 1) * halo, :] = wo_ref[...] + frac * add
        o_ref[(slabs + 1) * halo : (slabs + 2) * halo, :] = qo_ref[...]
        o_ref[(slabs + 2) * halo :, :] = frac

    (o1,) = call(
        edge_w,
        [(((slabs + 3) * halo, width), F32)],
        [re1, w_part, vo, weights, q_sent, frac_sent, q_o],
        flops=1e7,
    )
    ro1 = over_o(o1)

    def middle(v1_ref, v_ref, w_ref, pick_ref, sig_ref, frac_ref, wp_ref):
        va, vb = v1_ref[:elements, :], v1_ref[elements:, :]
        cut = split(va + vb)
        near = own_faces(faces, pick_ref, w_ref, [cut])[0]
        rest = v_ref[:elements, :] + v_ref[elements:, :] - DAMPING * product(cut, w_ref[W_DIAG])
        rest = rest / sig_ref[...] + product(split(va), w_ref[W_TIME]) + near
        wp_ref[...] = frac_ref[...] * rest + vb

    (wp,) = call(
        middle,
        [full],
        [v1, v0, weights, pick, sigma_all, frac_all],
        flops=1e9,
    )

    early_w = [later(wp, a) for a in range(1, groups)]

    def carry(v1_ref, v_ref, w_ref, sig_ref, x_ref):
        step = split(v1_ref[:elements, :] - v1_ref[elements:, :])
        x_ref[...] = v_ref[elements:, :] + sig_ref[...] * product(step, w_ref[W_TIME])

    (x_own,) = call(carry, [full], [v1, v0, weights, sigma_all], flops=1e8)

    few_rows = ((sent + halo, width), F32)

    def coarse_kernel(re_ref, ro_ref, vo_ref, w_ref, qs_ref, fracs_ref, w_out, table_ref):
        rows = arrived(re_ref, ro_ref.at[: slabs * halo, :], slabs)
        both = vo_ref[:halo, :] + vo_ref[halo:, :]
        rows.append(jnp.concatenate([both, both], axis=0))
        table = far_faces(faces, rows, w_ref)
        lanes = 2 * width
        add = spread(qs_ref[...], table[:, : slabs * lanes], slabs)
        late = fracs_ref[...] * (add[0] + add[1])
        even = lax.axis_index("space") % 2 == 0
        w_out[:halo, :] = jnp.where(even, late[halo:], late[:halo])
        w_out[halo:sent, :] = jnp.where(even, late[:halo], late[halo:])
        mine = spread(
            ro_ref[(slabs + 1) * halo : (slabs + 2) * halo, :].astype(BF16),
            table[:, slabs * lanes :],
            1,
        )[0]
        w_out[sent:, :] = (
            ro_ref[slabs * halo : (slabs + 1) * halo, :] + ro_ref[(slabs + 2) * halo :, :] * mine
        )
        table_ref[...] = table[:, : slabs * lanes]

    w_late, table1 = call(
        coarse_kernel,
        [few_rows, ((far, slabs * 2 * width), BF16)],
        [re1, ro1, vo, weights, q_sent, frac_sent],
        flops=1e7,
    )
    late_w = [later(w_late, a) for a in range(1, groups)]
    x_before = later(x_own, 1)

    def rest_kernel(
        table_ref, wp_ref, v1_ref, v_ref, w_ref, pick_ref, q_ref, sig_ref, frac_ref, sent_ref,
        pa_out, pb_out, ps_out, c_out,
    ):
        sigma = sig_ref[...]
        add = spread(q_ref[...], table_ref[...], slabs)
        va, vb = v1_ref[:elements, :], v1_ref[elements:, :]
        c_out[...] = wp_ref[...] - vb + frac_ref[...] * (add[0] + add[1])
        ca, cb = split(va), split(vb)
        ga, gb = own_faces(faces, pick_ref, w_ref, [ca, cb])
        a = va + v_ref[:elements, :] - DAMPING * product(ca, w_ref[W_DIAG])
        a = a + sigma * (ga + add[0])
        b = vb + v_ref[elements:, :] - DAMPING * product(cb, w_ref[W_DIAG])
        b = b + sigma * (product(ca, w_ref[W_TIME]) + gb + add[1])
        pa_out[...] = a
        pb_out[...] = b
        got = at_sent(sent_ref, [a, b])
        ps_out[:sent, :] = got[0]
        ps_out[sent:, :] = got[1]

    pa1, pb1, psent2, c_start = call(
        rest_kernel,
        [full, full, ((slabs * sent, width), F32), full],
        [table1, wp, v1, v0, weights, pick, q_all, sigma_all, frac_all, choose],
        flops=1e9,
    )

    def recur(*refs):
        n = groups - 1
        earlies, lates = refs[:n], refs[n : 2 * n]
        c0_ref, late_ref, ro_ref, w_ref, sent_ref, back_ref, frac_ref = refs[2 * n : 2 * n + 7]
        c_ref, d_ref, s_ref, e_ref, oh_ref = refs[2 * n + 7 :]
        every = jnp.concatenate([split(x[:sent, :]) for x in lates], axis=1)
        fixes = spread(back_ref[...], every, n)
        olds = [
            jnp.concatenate([x[...] + fix, y[sent:, :]], axis=0)
            for x, y, fix in zip(earlies, lates, fixes)
        ]
        frac = jnp.concatenate([frac_ref[...], ro_ref[(slabs + 2) * halo :, :]], axis=0)
        c = jnp.concatenate(
            [c0_ref[...], late_ref[sent:, :] - ro_ref[(slabs - 1) * halo : slabs * halo, :]], axis=0
        )
        d = time_mask(olds[0])
        power = frac
        for a in range(1, groups):
            cut = split(time_mask(power * olds[a - 1], a))
            c = c + product(cut, w_ref[W_TIME + a - 1])
            if a < groups - 1:
                cut = split(time_mask(power * olds[a], a + 1))
                d = d + product(cut, w_ref[W_TIME + a - 1])
                power = power * frac
        c_ref[...] = c[:elements]
        d_ref[...] = d[:elements]
        oh_ref[:halo, :] = c[elements:]
        oh_ref[halo:, :] = d[elements:]
        every = jnp.concatenate([split(c[:elements]), split(d[:elements])], axis=1)
        got = spread(sent_ref[...], every, 2)
        e_ref[:halo, :] = got[0][:halo]
        e_ref[halo:, :] = got[1][:halo]
        s_ref[:sent, :] = got[0]
        s_ref[sent:, :] = got[1]

    c_all, d_all, cd_sent, e2, ro2 = call(
        recur,
        [full, full, ((2 * sent, width), F32), edge, edge],
        [*early_w, *late_w, c_start, w_late, ro1, weights, choose, put_back, frac_all],
        flops=1e8,
    )
    re2 = over_e(e2)

    def ahead_two(c_ref, cds_ref, ps_ref, w_ref, picks_ref, sigs_ref, out_ref):
        sigma = sigs_ref[...]
        near = sent_faces(picks_ref, w_ref, split(c_ref[...]), 0)
        c = cds_ref[:sent, :]
        same = c - DAMPING * few(c, w_ref.at[W_DIAG]) + sigma * near
        times = few(cds_ref[...], w_ref.at[W_TIME])
        out_ref[:sent, :] = ps_ref[:sent, :] + same + sigma * times[sent:]
        out_ref[sent:, :] = ps_ref[sent:, :] + same + sigma * times[:sent]

    (psent3,) = call(
        ahead_two,
        [((slabs * sent, width), F32)],
        [c_all, cd_sent, psent2, weights, pick_sent, sig_sent],
        flops=1e8,
    )

    def near_c(c_ref, w_ref, pick_ref, g_ref):
        g_ref[...] = own_faces(faces, pick_ref, w_ref, [split(c_ref[...])])[0]

    (g_c,) = call(near_c, [full], [c_all, weights, pick], flops=3e8)

    def edge_two(re_ref, ro_ref, psent_ref, sigs_ref, w_ref, qs_ref, e_ref, o_ref):
        table = far_faces(faces, arrived(re_ref, ro_ref, 2)[:1], w_ref)
        add = sigs_ref[...] * spread(qs_ref[...], table, 1)[0]
        put_sent(
            e_ref, o_ref, [psent_ref[t * sent : (t + 1) * sent, :] + add for t in range(slabs)]
        )

    e3, o3 = call(
        edge_two,
        [edge, edge],
        [re2, ro2, psent3, sig_sent, weights, q_sent],
        flops=1e7,
    )
    re3, ro3 = over_e(e3), over_o(o3)

    def sweep(
        re_ref, ro_ref, c_in, d_in, g_ref, xb_ref, pa_ref, pb_ref, v_ref, w_ref, pick_ref, q_ref, sig_ref,
        out_ref,
    ):
        sigma = sig_ref[...]
        c, d = c_in[...], d_in[...]
        cc, cd = split(c), split(d)
        gc, gd = g_ref[...], own_faces(faces, pick_ref, w_ref, [cd])[0]
        add = spread(q_ref[...], far_faces(faces, arrived(re_ref, ro_ref, 2), w_ref), 2)
        same = c - DAMPING * product(cc, w_ref[W_DIAG]) + sigma * (gc + add[0])
        td = product(cd, w_ref[W_TIME])
        a = pa_ref[...] + same + sigma * td
        b = pb_ref[...] + same + sigma * product(cc, w_ref[W_TIME])
        z = (
            time_mask(xb_ref[...])
            + d
            - DAMPING * product(cd, w_ref[W_DIAG])
            + sigma * (td + gd + add[1])
        )
        ca, cb = split(a), split(b)
        ga, gb = own_faces(faces, pick_ref, w_ref, [ca, cb])
        tz, ta = product(split(z), w_ref[W_TIME]), product(ca, w_ref[W_TIME])
        out_ref[:elements, :] = (
            a + v_ref[:elements, :] - DAMPING * product(ca, w_ref[W_DIAG]) + sigma * (tz + ga)
        )
        out_ref[elements:, :] = (
            b + v_ref[elements:, :] - DAMPING * product(cb, w_ref[W_DIAG]) + sigma * (ta + gb)
        )

    (part4,) = call(
        sweep,
        [two],
        [re2, ro2, c_all, d_all, g_c, x_before, pa1, pb1, v0, weights, pick, q_all, sigma_all],
        flops=2e9,
    )

    def last(re_ref, ro_ref, p_ref, w_ref, q_ref, sig_ref, out_hbm, out_ref, sems):
        table = far_faces(faces, arrived(re_ref, ro_ref, slabs), w_ref)
        lanes = 2 * width
        copies = []
        for t in range(slabs):
            rows = pl.ds(t * elements, elements)
            add = spread(q_ref[...], table[:, t * lanes : (t + 1) * lanes], 1)[0]
            out_ref[t * elements : (t + 1) * elements, :] = (
                p_ref[t * elements : (t + 1) * elements, :] + sig_ref[...] * add
            )
            copies.append(
                pltpu.make_async_copy(out_ref.at[rows, :], out_hbm.at[rows, :], sems.at[t])
            )
            copies[-1].start()
        for c in copies:
            c.wait()

    (out,) = call(
        last,
        [two],
        [re3, ro3, part4, weights, q_all, sigma_all],
        scratch=[VMEM((slabs * elements, width), F32), pltpu.SemaphoreType.DMA((slabs,))],
        flops=1e7,
        out_space=HBM,
    )
    return out.reshape(slabs, elements, width)


def solution(mesh):
    in_specs = (
        P("tm", "space", None),
        P("space"),
        P(),
        P(),
        P(),
        P(),
        P("space", None),
        P("space", None),
    )
    out_specs = P("tm", "space", None)
    return jax.shard_map(body, mesh=mesh, in_specs=in_specs, out_specs=out_specs, check_vma=False)
```

```python
import jax
import jax.numpy as jnp
from jax import lax
from jax.experimental import pallas as pl
from jax.experimental.pallas import tpu as pltpu
from jax.sharding import PartitionSpec as P


DAMPING = 0.7
F32 = jnp.float32
BF16 = jnp.bfloat16
VMEM = pltpu.VMEM
SMEM = pltpu.SMEM
HBM = pltpu.MemorySpace.HBM

W_DIAG, W_FACE, W_SOURCE_TIME, W_TIME = 0, 1, 5, 6


def call(kernel, out_shapes, args, spaces=None, scratch=(), flops=4e8, out_space=VMEM):
    spaces = spaces or [VMEM] * len(args)
    args = [
        pltpu.with_memory_space_constraint(x, HBM) if s is HBM else x for x, s in zip(args, spaces)
    ]
    return pl.pallas_call(
        kernel,
        out_shape=[jax.ShapeDtypeStruct(s, d) for s, d in out_shapes],
        in_specs=[pl.BlockSpec(memory_space=s) for s in spaces],
        out_specs=[pl.BlockSpec(memory_space=out_space)] * len(out_shapes),
        scratch_shapes=list(scratch),
        compiler_params=pltpu.CompilerParams(vmem_limit_bytes=24 << 20),
        cost_estimate=pl.CostEstimate(flops=int(flops), bytes_accessed=1 << 20, transcendentals=0),
    )(*args)


def fetch(pairs, sems):
    copies = [pltpu.make_async_copy(a, b, sems.at[i]) for i, (a, b) in enumerate(pairs)]
    for c in copies:
        c.start()
    return copies


def split(x):
    head = x.astype(BF16)
    tail = (x - head.astype(F32)).astype(BF16)
    return jnp.concatenate([head, tail], axis=1)


def halves(x):
    width = x.shape[1] // 2
    return x[:, :width] + x[:, width:]


def dot(left, right):
    return jnp.dot(left, right, preferred_element_type=F32)


def dot32(left, right):
    return jnp.dot(left, right, precision=lax.Precision.HIGHEST, preferred_element_type=F32)


def product(parts, tile):
    return halves(dot(parts, tile))


def few(x, tile):
    head = x.astype(BF16)
    tail = (x - head.astype(F32)).astype(BF16)
    out = halves(dot(jnp.concatenate([head, tail], axis=0), tile[: x.shape[1], :]))
    return out[: x.shape[0]] + out[x.shape[0] :]


def weight_tile(w):
    head = w.astype(BF16)
    tail = (w - head.astype(F32)).astype(BF16)
    top = jnp.concatenate([head, tail], axis=1)
    low = jnp.concatenate([head, jnp.zeros_like(head)], axis=1)
    return jnp.concatenate([top, low], axis=0)


def column(row, width):
    return jnp.transpose(jnp.broadcast_to(row, (width, row.shape[1])))


def own_faces(faces, pick_ref, weights_ref, parts):
    count = len(parts)
    width = parts[0].shape[1]
    rows = parts[0].shape[0]
    every = jnp.concatenate(parts, axis=1) if count > 1 else parts[0]
    sums = [None] * count
    for face in range(faces):
        picked = dot(pick_ref[face * rows : (face + 1) * rows, :], every).astype(BF16)
        for i in range(count):
            term = dot(picked[:, i * width : (i + 1) * width], weights_ref[W_FACE + face])
            sums[i] = term if sums[i] is None else sums[i] + term
    return [halves(s) for s in sums]


def arrived(from_e, from_o, count):
    even = lax.axis_index("space") % 2 == 0
    left = jnp.where(even, from_o[...], from_e[...])
    right = jnp.where(even, from_e[...], from_o[...])
    rows = left.shape[0] // count
    return [
        jnp.concatenate([left[i * rows : (i + 1) * rows], right[i * rows : (i + 1) * rows]], axis=0)
        for i in range(count)
    ]


def far_faces(faces, rows_in, weights_ref):
    count = len(rows_in)
    n = rows_in[0].shape[0]
    rows = jnp.concatenate(rows_in, axis=0) if count > 1 else rows_in[0]
    per_face = [few(rows, weights_ref.at[W_FACE + f]) for f in range(faces)]
    lanes = [
        split(jnp.concatenate([u[i * n : (i + 1) * n] for u in per_face], axis=0))
        for i in range(count)
    ]
    return jnp.concatenate(lanes, axis=1) if count > 1 else lanes[0]


def spread(select, table, count):
    total = dot(select, table)
    width = total.shape[1] // count
    return [halves(total[:, i * width : (i + 1) * width]) for i in range(count)]


def put_sent(e_ref, o_ref, slabs):
    rows = slabs[0].shape[0] // 2
    for i, s in enumerate(slabs):
        e_ref[i * rows : (i + 1) * rows, :] = s[:rows]
        o_ref[i * rows : (i + 1) * rows, :] = s[rows:]


def at_sent(sent_ref, values):
    every = jnp.concatenate([split(v) for v in values], axis=1)
    return spread(sent_ref[...], every, len(values))


def body(
    source, elem_scale, diag_block, block_inverse, face_flux, time_trace, neighbours, send_rows
):
    slabs, elements, width = source.shape
    faces = neighbours.shape[1]
    sent = send_rows.shape[1]
    halo = sent // 2
    groups = lax.axis_size("tm")
    ring = lax.axis_size("space")
    flat = source.reshape(slabs * elements, width)
    scale_row = elem_scale.reshape(1, elements)
    faces_row = neighbours.T
    stack = W_TIME + groups - 1
    full = ((elements, width), F32)
    two = ((slabs * elements, width), F32)
    edge = ((slabs * halo, width), F32)
    far = faces * sent

    swap_e = [(i, i ^ 1) for i in range(ring)]
    swap_o = [(i, (i + 1) % ring if i % 2 else (i - 1) % ring) for i in range(ring)]

    def over_e(x):
        return lax.ppermute(x, "space", swap_e)

    def over_o(x):
        return lax.ppermute(x, "space", swap_o)

    def later(x, by):
        return lax.ppermute(x, "tm", [(i, (i + by) % groups) for i in range(groups)])

    def sent_faces(picks_ref, w_ref, parts, start):
        near = None
        for f in range(faces):
            picked = dot(picks_ref[f * sent + start : (f + 1) * sent, :], parts).astype(BF16)
            term = dot(picked, w_ref[W_FACE + f])
            near = term if near is None else near + term
        return halves(near)

    def unpacked(block):
        even = lax.axis_index("space") % 2 == 0
        low = lax.broadcasted_iota(jnp.int32, block.shape, 1) % sent < halo
        kept = jnp.where(low, jnp.where(even, 0.0, 1.0), jnp.where(even, 1.0, 0.0))
        factor = jnp.where(even, block[:, :1], block[:, halo : halo + 1])
        return (block * kept).astype(BF16), jnp.broadcast_to(factor, (halo, width))

    def sent_at(send_ref, i):
        first = jnp.where(lax.axis_index("space") % 2 == 0, halo, 0)
        return send_ref[0, lax.rem(first + i, sent)]

    pieces = 2
    piece = elements // pieces

    def first_kernel(
        s_hbm, scale_hbm, inv_hbm, send_hbm, d_hbm, f_hbm, t_hbm, nbr_hbm,
        e_ref, o_ref, xa_ref, xb_ref, col_ref, inv_ref, fold_ref, nbr_ref,
        s_ref, scale_ref, send_ref, g_ref, sems,
    ):
        parts = [pl.ds(i * piece, piece) for i in range(slabs * pieces)]
        pairs = [(scale_hbm, scale_ref), (send_hbm, send_ref)]
        pairs += [(s_hbm.at[p, :], s_ref.at[p, :]) for p in parts]
        pairs += [
            (inv_hbm, inv_ref),
            (d_hbm, fold_ref.at[:width, :]),
            (f_hbm, fold_ref.at[width : (faces + 1) * width, :]),
            (t_hbm, fold_ref.at[(faces + 1) * width :, :]),
            (nbr_hbm, nbr_ref),
        ]
        copies = fetch(pairs, sems)
        copies[0].wait()
        scale = column(scale_ref[...], width)
        col_ref[...] = scale
        sigma = DAMPING / scale
        for c in copies[1 : 2 + slabs * pieces]:
            c.wait()
        refs = [xa_ref, xb_ref]
        for t in range(slabs):
            refs[t][...] = s_ref[t * elements : (t + 1) * elements, :] * sigma
        for i in range(sent):
            at = sent_at(send_ref, i)
            base = (i // halo) * slabs * halo + i % halo
            for t in range(slabs):
                g_ref[base + t * halo : base + t * halo + 1, :] = refs[t][pl.ds(at, 1), :]
        copies[2 + slabs * pieces].wait()
        out = dot32(g_ref[...], inv_ref[...])
        e_ref[...] = out[: slabs * halo]
        o_ref[...] = out[slabs * halo :]
        for c in copies[3 + slabs * pieces :]:
            c.wait()

    e0, o0, xa, xb, scale_col, inv_here, fold, faces_here = call(
        first_kernel,
        [
            edge, edge, full, full, full, ((width, width), F32),
            (((faces + 2) * width, width), F32), ((faces, elements), jnp.int32),
        ],
        [
            flat, scale_row, block_inverse, send_rows, diag_block,
            face_flux.reshape(faces * width, width), time_trace, faces_row,
        ],
        spaces=[HBM] * 8,
        scratch=[
            VMEM((slabs * elements, width), F32),
            VMEM((1, elements), F32),
            SMEM((1, sent), jnp.int32),
            VMEM((slabs * sent, width), F32),
            pltpu.SemaphoreType.DMA((slabs * pieces + 7,)),
        ],
        flops=1e7,
    )
    before = later(xb, 1)
    re0, ro0 = over_e(e0), over_o(o0)

    def setup_kernel(
        xa_ref, xb_ref, col_ref, inv_ref, fold_ref, nbr_ref, send_hbm,
        v_ref, part_ref, psent_ref, sigs_ref, fracs_ref, w_ref, pick_ref, picks_ref, q_ref, qs_ref,
        qo_ref, sent_ref, back_ref, sig_ref, frac_ref,
        send_ref, line_ref, rows_ref, sems,
    ):
        copies = fetch([(send_hbm, send_ref), (send_hbm, line_ref)], sems)
        head = weight_tile(inv_ref[...])
        folded = product(split(fold_ref[...]), head)
        for i in range(faces + 1):
            w_ref[W_DIAG + i] = weight_tile(folded[i * width : (i + 1) * width])
        trace = folded[(faces + 1) * width :]
        step = weight_tile(trace)
        w_ref[W_TIME] = step
        power = trace
        for a in range(1, groups - 1):
            if a == 1:
                both = product(split(jnp.concatenate([inv_ref[...], trace], axis=0)), step)
                w_ref[W_SOURCE_TIME] = weight_tile(both[:width])
                power = both[width:]
            else:
                power = product(split(power), step)
            w_ref[W_TIME + a] = weight_tile(power)
        if groups < 3:
            w_ref[W_SOURCE_TIME] = weight_tile(product(split(inv_ref[...]), step))
        scale = col_ref[...]
        sigma = DAMPING / scale
        sig_ref[...] = sigma
        frac = 1.0 / (2.0 * scale - 1.0)
        frac_ref[...] = frac
        lane = lax.broadcasted_iota(jnp.int32, (elements, far), 1)
        spot = lax.broadcasted_iota(jnp.int32, (elements, far), 1)
        wanted = jnp.zeros((elements, far), jnp.int32)
        for f in range(faces):
            wide = column(nbr_ref[f : f + 1, :], far)
            for base in range(0, elements, far):
                pick_ref[f * elements : (f + 1) * elements, base : base + far] = jnp.where(
                    wide == lane + base, 1.0, 0.0
                ).astype(BF16)
            wanted = jnp.where(spot // sent == f, wide, wanted)
        q = jnp.where(wanted == elements + spot % sent, 1.0, 0.0).astype(BF16)
        q_ref[...] = q
        strip = lax.broadcasted_iota(jnp.int32, (1, elements), 1)
        for c in copies:
            c.wait()
        row = lax.broadcasted_iota(jnp.int32, (elements, sent), 0)
        back_ref[...] = jnp.where(row == line_ref[...], 1.0, 0.0).astype(BF16)
        for i in range(sent):
            rows_ref[i : i + 1, :] = jnp.where(strip == sent_at(send_ref, i), 1.0, 0.0)
        chosen = rows_ref[...].astype(BF16)
        sent_ref[...] = chosen
        qs = dot(chosen, q)
        qs_ref[...] = qs.astype(BF16)
        for f in range(faces):
            picks_ref[f * sent : (f + 1) * sent, :] = dot(
                chosen, pick_ref[f * elements : (f + 1) * elements, :]
            ).astype(BF16)
        v = [product(split(x[...]), head) for x in (xa_ref, xb_ref)]
        cut = [split(x) for x in v]
        near = own_faces(faces, pick_ref, w_ref, cut)
        parts = []
        for t in range(slabs):
            term = near[t]
            if t:
                term = term + product(cut[t - 1], w_ref[W_TIME])
            parts.append(
                2.0 * v[t] - DAMPING * product(cut[t], w_ref[W_DIAG]) + sigma * term
            )
            v_ref[t * elements : (t + 1) * elements, :] = v[t]
            part_ref[t * elements : (t + 1) * elements, :] = parts[t]
        got = at_sent(sent_ref, parts + [sigma, frac])
        for t in range(slabs):
            psent_ref[t * sent : (t + 1) * sent, :] = got[t]
        sigs_ref[...] = got[slabs]
        fracs_ref[...] = got[slabs + 1]
        near_half = lax.broadcasted_iota(jnp.int32, (halo, far), 1) % sent < halo
        even = lax.axis_index("space") % 2 == 0
        kept = jnp.where(near_half, jnp.where(even, 1.0, 0.0), jnp.where(even, 0.0, 1.0))
        qo_ref[...] = qs[halo:] * kept + got[slabs + 1][halo:] * (1.0 - kept)

    (
        v0, part1, psent1, sig_sent, frac_sent, weights, pick, pick_sent, q_all, q_sent, q_o, choose,
        put_back, sigma_all, frac_all,
    ) = call(
        setup_kernel,
        [
            two, two, ((slabs * sent, width), F32), ((sent, width), F32), ((sent, width), F32),
            ((stack, 2 * width, 2 * width), BF16), ((faces * elements, elements), BF16),
            ((faces * sent, elements), BF16), ((elements, far), BF16), ((sent, far), BF16),
            ((halo, far), F32), ((sent, elements), BF16), ((elements, sent), BF16), full, full,
        ],
        [
            xa, xb, scale_col, inv_here, fold, faces_here, send_rows,
        ],
        spaces=[VMEM] * 6 + [HBM],
        scratch=[
            SMEM((1, sent), jnp.int32),
            VMEM((1, sent), jnp.int32),
            VMEM((sent, elements), F32),
            pltpu.SemaphoreType.DMA((2,)),
        ],
        flops=2e9,
    )

    def time_mask(x, by=1):
        return jnp.where(lax.axis_index("tm") >= by, x, jnp.zeros_like(x))

    def edge_one(
        re_ref, ro_ref, b_ref, psent_ref, sigs_ref, w_ref, qs_ref, sent_ref, e_ref, o_ref
    ):
        table = far_faces(faces, arrived(re_ref, ro_ref, slabs), w_ref)
        add = spread(qs_ref[...], table, slabs)
        picked = dot(sent_ref[...], split(b_ref[...])).astype(BF16)
        old = time_mask(product(picked, w_ref[W_SOURCE_TIME]))
        sig = sigs_ref[...]
        new = [psent_ref[t * sent : (t + 1) * sent, :] + sig * add[t] for t in range(slabs)]
        new[0] = new[0] + sig * old
        put_sent(e_ref, o_ref, new)

    e1, vo = call(
        edge_one,
        [edge, edge],
        [re0, ro0, before, psent1, sig_sent, weights, q_sent, choose],
        flops=1e7,
    )
    re1 = over_e(e1)

    def ahead(
        re_ref, ro_ref, b_ref, part_ref, vo_ref, o0_ref, w_ref, picks_ref, q_ref, sig_ref,
        sigs_ref, fracs_ref, v1_ref, wo_ref,
    ):
        sigma = sig_ref[...]
        add = spread(q_ref[...], far_faces(faces, arrived(re_ref, ro_ref, slabs), w_ref), slabs)
        old = time_mask(product(split(b_ref[...]), w_ref[W_SOURCE_TIME]))
        va = part_ref[:elements, :] + sigma * add[0] + sigma * old
        vb = part_ref[elements:, :] + sigma * add[1]
        v1_ref[:elements, :] = va
        v1_ref[elements:, :] = vb
        near = sent_faces(picks_ref, w_ref, split(va + vb), halo)
        sa, sb = vo_ref[:halo, :], vo_ref[halo:, :]
        rest = (
            o0_ref[:halo, :] + o0_ref[halo:, :] - DAMPING * few(sa + sb, w_ref.at[W_DIAG])
        ) / sigs_ref[halo:, :]
        rest = rest + few(sa, w_ref.at[W_TIME]) + near
        wo_ref[...] = fracs_ref[halo:, :] * rest + sb

    v1, w_part = call(
        ahead,
        [two, ((halo, width), F32)],
        [
            re0, ro0, before, part1, vo, o0, weights, pick_sent, q_all, sigma_all, sig_sent,
            frac_sent,
        ],
        flops=2e8,
    )

    def edge_w(re_ref, wo_ref, vo_ref, w_ref, qs_ref, fracs_ref, qo_ref, o_ref):
        both = re_ref[:halo, :] + re_ref[halo:, :]
        none = jnp.zeros_like(both)
        even = lax.axis_index("space") % 2 == 0
        rows = jnp.concatenate([jnp.where(even, none, both), jnp.where(even, both, none)], axis=0)
        add = spread(qs_ref[halo:, :], far_faces(faces, [rows], w_ref), 1)[0]
        frac = fracs_ref[halo:, :]
        o_ref[: slabs * halo, :] = vo_ref[...]
        o_ref[slabs * halo : (slabs + 1) * halo, :] = wo_ref[...] + frac * add
        o_ref[(slabs + 1) * halo :, :] = qo_ref[...]

    (o1,) = call(
        edge_w,
        [(((slabs + 2) * halo, width), F32)],
        [re1, w_part, vo, weights, q_sent, frac_sent, q_o],
        flops=1e7,
    )
    ro1 = over_o(o1)

    def middle(v1_ref, v_ref, w_ref, pick_ref, sig_ref, frac_ref, wp_ref):
        va, vb = v1_ref[:elements, :], v1_ref[elements:, :]
        cut = split(va + vb)
        near = own_faces(faces, pick_ref, w_ref, [cut])[0]
        rest = v_ref[:elements, :] + v_ref[elements:, :] - DAMPING * product(cut, w_ref[W_DIAG])
        rest = rest / sig_ref[...] + product(split(va), w_ref[W_TIME]) + near
        wp_ref[...] = frac_ref[...] * rest + vb

    (wp,) = call(
        middle,
        [full],
        [v1, v0, weights, pick, sigma_all, frac_all],
        flops=1e9,
    )

    early_w = [later(wp, a) for a in range(1, groups)]

    def carry(v1_ref, v_ref, w_ref, sig_ref, x_ref):
        step = split(v1_ref[:elements, :] - v1_ref[elements:, :])
        x_ref[...] = v_ref[elements:, :] + sig_ref[...] * product(step, w_ref[W_TIME])

    (x_own,) = call(carry, [full], [v1, v0, weights, sigma_all], flops=1e8)

    few_rows = ((sent + halo, width), F32)

    def coarse_kernel(re_ref, ro_ref, vo_ref, w_ref, qs_ref, fracs_ref, w_out, table_ref):
        rows = arrived(re_ref, ro_ref.at[: slabs * halo, :], slabs)
        both = vo_ref[:halo, :] + vo_ref[halo:, :]
        rows.append(jnp.concatenate([both, both], axis=0))
        table = far_faces(faces, rows, w_ref)
        lanes = 2 * width
        add = spread(qs_ref[...], table[:, : slabs * lanes], slabs)
        late = fracs_ref[...] * (add[0] + add[1])
        even = lax.axis_index("space") % 2 == 0
        w_out[:halo, :] = jnp.where(even, late[halo:], late[:halo])
        w_out[halo:sent, :] = jnp.where(even, late[:halo], late[halo:])
        chosen, factor = unpacked(ro_ref[(slabs + 1) * halo :, :])
        mine = spread(chosen, table[:, slabs * lanes :], 1)[0]
        w_out[sent:, :] = ro_ref[slabs * halo : (slabs + 1) * halo, :] + factor * mine
        table_ref[...] = table[:, : slabs * lanes]

    w_late, table1 = call(
        coarse_kernel,
        [few_rows, ((far, slabs * 2 * width), BF16)],
        [re1, ro1, vo, weights, q_sent, frac_sent],
        flops=1e7,
    )
    late_w = [later(w_late, a) for a in range(1, groups)]
    x_before = later(x_own, 1)

    def rest_kernel(
        table_ref, wp_ref, v1_ref, v_ref, w_ref, pick_ref, q_ref, sig_ref, frac_ref, sent_ref,
        pa_out, pb_out, ps_out, c_out,
    ):
        sigma = sig_ref[...]
        add = spread(q_ref[...], table_ref[...], slabs)
        va, vb = v1_ref[:elements, :], v1_ref[elements:, :]
        c_out[...] = wp_ref[...] - vb + frac_ref[...] * (add[0] + add[1])
        ca, cb = split(va), split(vb)
        ga, gb = own_faces(faces, pick_ref, w_ref, [ca, cb])
        a = va + v_ref[:elements, :] - DAMPING * product(ca, w_ref[W_DIAG])
        a = a + sigma * (ga + add[0])
        b = vb + v_ref[elements:, :] - DAMPING * product(cb, w_ref[W_DIAG])
        b = b + sigma * (product(ca, w_ref[W_TIME]) + gb + add[1])
        pa_out[...] = a
        pb_out[...] = b
        got = at_sent(sent_ref, [a, b])
        ps_out[:sent, :] = got[0]
        ps_out[sent:, :] = got[1]

    pa1, pb1, psent2, c_start = call(
        rest_kernel,
        [full, full, ((slabs * sent, width), F32), full],
        [table1, wp, v1, v0, weights, pick, q_all, sigma_all, frac_all, choose],
        flops=1e9,
    )

    def recur(*refs):
        n = groups - 1
        earlies, lates = refs[:n], refs[n : 2 * n]
        c0_ref, late_ref, ro_ref, w_ref, sent_ref, back_ref, frac_ref = refs[2 * n : 2 * n + 7]
        c_ref, d_ref, s_ref, e_ref, oh_ref = refs[2 * n + 7 :]
        every = jnp.concatenate([split(x[:sent, :]) for x in lates], axis=1)
        fixes = spread(back_ref[...], every, n)
        olds = [
            jnp.concatenate([x[...] + fix, y[sent:, :]], axis=0)
            for x, y, fix in zip(earlies, lates, fixes)
        ]
        frac = jnp.concatenate(
            [frac_ref[...], unpacked(ro_ref[(slabs + 1) * halo :, :])[1]], axis=0
        )
        c = jnp.concatenate(
            [c0_ref[...], late_ref[sent:, :] - ro_ref[(slabs - 1) * halo : slabs * halo, :]], axis=0
        )
        d = time_mask(olds[0])
        power = frac
        for a in range(1, groups):
            cut = split(time_mask(olds[a - 1], a))
            if a > 1:
                d = d + power * product(cut, w_ref[W_TIME + a - 2])
                power = power * frac
            c = c + power * product(cut, w_ref[W_TIME + a - 1])
        c_ref[...] = c[:elements]
        d_ref[...] = d[:elements]
        oh_ref[:halo, :] = c[elements:]
        oh_ref[halo:, :] = d[elements:]
        every = jnp.concatenate([split(c[:elements]), split(d[:elements])], axis=1)
        got = spread(sent_ref[...], every, 2)
        e_ref[:halo, :] = got[0][:halo]
        e_ref[halo:, :] = got[1][:halo]
        s_ref[:sent, :] = got[0]
        s_ref[sent:, :] = got[1]

    c_all, d_all, cd_sent, e2, ro2 = call(
        recur,
        [full, full, ((2 * sent, width), F32), edge, edge],
        [*early_w, *late_w, c_start, w_late, ro1, weights, choose, put_back, frac_all],
        flops=1e8,
    )
    re2 = over_e(e2)

    def ahead_two(c_ref, cds_ref, ps_ref, w_ref, picks_ref, sigs_ref, out_ref):
        sigma = sigs_ref[...]
        near = sent_faces(picks_ref, w_ref, split(c_ref[...]), 0)
        c = cds_ref[:sent, :]
        same = c - DAMPING * few(c, w_ref.at[W_DIAG]) + sigma * near
        times = few(cds_ref[...], w_ref.at[W_TIME])
        out_ref[:sent, :] = ps_ref[:sent, :] + same + sigma * times[sent:]
        out_ref[sent:, :] = ps_ref[sent:, :] + same + sigma * times[:sent]

    (psent3,) = call(
        ahead_two,
        [((slabs * sent, width), F32)],
        [c_all, cd_sent, psent2, weights, pick_sent, sig_sent],
        flops=1e8,
    )

    def near_c(c_ref, w_ref, pick_ref, g_ref):
        g_ref[...] = own_faces(faces, pick_ref, w_ref, [split(c_ref[...])])[0]

    (g_c,) = call(near_c, [full], [c_all, weights, pick], flops=3e8)

    def edge_two(re_ref, ro_ref, psent_ref, sigs_ref, w_ref, qs_ref, e_ref, o_ref):
        table = far_faces(faces, arrived(re_ref, ro_ref, 2)[:1], w_ref)
        add = sigs_ref[...] * spread(qs_ref[...], table, 1)[0]
        put_sent(
            e_ref, o_ref, [psent_ref[t * sent : (t + 1) * sent, :] + add for t in range(slabs)]
        )

    e3, o3 = call(
        edge_two,
        [edge, edge],
        [re2, ro2, psent3, sig_sent, weights, q_sent],
        flops=1e7,
    )
    re3, ro3 = over_e(e3), over_o(o3)

    def sweep(
        re_ref, ro_ref, c_in, d_in, g_ref, xb_ref, pa_ref, pb_ref, v_ref, w_ref, pick_ref, q_ref, sig_ref,
        out_ref,
    ):
        sigma = sig_ref[...]
        c, d = c_in[...], d_in[...]
        cc, cd = split(c), split(d)
        gc, gd = g_ref[...], own_faces(faces, pick_ref, w_ref, [cd])[0]
        add = spread(q_ref[...], far_faces(faces, arrived(re_ref, ro_ref, 2), w_ref), 2)
        same = c - DAMPING * product(cc, w_ref[W_DIAG]) + sigma * (gc + add[0])
        td = product(cd, w_ref[W_TIME])
        a = pa_ref[...] + same + sigma * td
        b = pb_ref[...] + same + sigma * product(cc, w_ref[W_TIME])
        z = (
            time_mask(xb_ref[...])
            + d
            - DAMPING * product(cd, w_ref[W_DIAG])
            + sigma * (td + gd + add[1])
        )
        ca, cb = split(a), split(b)
        ga, gb = own_faces(faces, pick_ref, w_ref, [ca, cb])
        tz, ta = product(split(z), w_ref[W_TIME]), product(ca, w_ref[W_TIME])
        out_ref[:elements, :] = (
            a + v_ref[:elements, :] - DAMPING * product(ca, w_ref[W_DIAG]) + sigma * (tz + ga)
        )
        out_ref[elements:, :] = (
            b + v_ref[elements:, :] - DAMPING * product(cb, w_ref[W_DIAG]) + sigma * (ta + gb)
        )

    (part4,) = call(
        sweep,
        [two],
        [re2, ro2, c_all, d_all, g_c, x_before, pa1, pb1, v0, weights, pick, q_all, sigma_all],
        flops=2e9,
    )

    def last(re_ref, ro_ref, p_ref, w_ref, q_ref, sig_ref, out_hbm, out_ref, sems):
        table = far_faces(faces, arrived(re_ref, ro_ref, slabs), w_ref)
        lanes = 2 * width
        copies = []
        for t in range(slabs):
            rows = pl.ds(t * elements, elements)
            add = spread(q_ref[...], table[:, t * lanes : (t + 1) * lanes], 1)[0]
            out_ref[t * elements : (t + 1) * elements, :] = (
                p_ref[t * elements : (t + 1) * elements, :] + sig_ref[...] * add
            )
            copies.append(
                pltpu.make_async_copy(out_ref.at[rows, :], out_hbm.at[rows, :], sems.at[t])
            )
            copies[-1].start()
        for c in copies:
            c.wait()

    (out,) = call(
        last,
        [two],
        [re3, ro3, part4, weights, q_all, sigma_all],
        scratch=[VMEM((slabs * elements, width), F32), pltpu.SemaphoreType.DMA((slabs,))],
        flops=1e7,
        out_space=HBM,
    )
    return out.reshape(slabs, elements, width)


def solution(mesh):
    in_specs = (
        P("tm", "space", None),
        P("space"),
        P(),
        P(),
        P(),
        P(),
        P("space", None),
        P("space", None),
    )
    out_specs = P("tm", "space", None)
    return jax.shard_map(body, mesh=mesh, in_specs=in_specs, out_specs=out_specs, check_vma=False)
```
